128 devices in a mesh: req: 64 (over z, y, x), tp: 2 (over core).
Axes of the slice: x: 4, y: 4, z: 4, core: 2. Of those that a mesh axis runs over, the one named last changes fastest.
Arguments:
- patches: bfloat16 [16384, 1664], P('req', 'tp'), may hold values from -6 to 6
- segment: int32 [16384], P('req'), may hold values from 0 to 2, as said below
- owner: int32 [128], P('req'), may hold values from 0 to 63, as said below
- w_qkv: bfloat16 [3, 1664, 1664], P(None, None, 'tp'), as said below
- w_out: bfloat16 [1664, 1664], P('tp'), may hold values from -0.15625 to 0.15625
- w_up: bfloat16 [1664, 8192], P(None, 'tp'), may hold values from -0.15625 to 0.15625
- w_down: bfloat16 [8192, 1664], P('tp'), may hold values from -0.0625 to 0.0625
- gains: float32 [3, 1664], replicated, may hold values from 0.1 to 1.9
- w_merge: bfloat16 [6656, 4096], P(None, 'tp'), may hold values from -0.078125 to 0.078125
Outputs:
- routed: bfloat16 [4096, 4096], P('req', 'tp')
The draws below stay inside these ranges and needn't reach their ends.
Inputs may be any that keep to these rules, and one draw needn't show every extreme that they name: On each shard the requests 0 to 1 lie in order from slot 0, request j filling 4 c_j consecutive slots with c_j from 1 to 32 merged rows, one request of every shard exactly 32; the remaining slots are padding with segment 2. `owner`: owners of the requests of one shard are all different; every device owns exactly one request of each index j from 0 to 1 among all shards. `w_qkv`: Real-valued projections of order one in their products, with no further structure promised.
All inputs are finite; a program needn't handle non-finite values.
Results may differ from the reference program's by a relative error of at most 0.018.
Values may be sent and summed in bfloat16 or wider, within the bound.
A program may use at most 192 MiB of HBM per device.

```python
import jax
import jax.numpy as jnp
from jax import lax

D = 1664
HEADS = 16
HEAD_DIM = 104
FF = 8192
OUT = 4096
CAP = 32
TOK_DEV = 256
R_DEV = 2
TOKENS = 16384
N_REQ = 64


def request_layout(key):
    shards = TOKENS // TOK_DEV
    count_key, big_key = jax.random.split(jax.random.fold_in(key, 11))
    counts = jax.random.randint(count_key, (shards, R_DEV), 1, CAP + 1)
    biggest = jax.random.randint(big_key, (shards,), 0, R_DEV)
    counts = jnp.where(jnp.arange(R_DEV)[None, :] == biggest[:, None], CAP, counts)
    return counts


def draw_segment(key, part):
    counts = request_layout(key)
    ends = jnp.cumsum(4 * counts, axis=1)
    places = jnp.arange(TOK_DEV)
    labels = jnp.sum(places[None, :, None] >= ends[:, None, :], axis=2).astype(jnp.int32)
    return labels.reshape(-1)


def draw_owner(key, part):
    shards = TOKENS // TOK_DEV
    perm_key = jax.random.fold_in(key, 23)
    order = jax.random.permutation(perm_key, shards)
    place = (jnp.arange(shards)[:, None] + jnp.arange(R_DEV)[None, :]) % shards
    result = order[place]
    return result.astype(jnp.int32).reshape(-1)


def draw_w_qkv(key, part):
    base = jax.random.normal(key, (3, D, D), jnp.float32) * D ** (-0.5)
    return base.astype(jnp.bfloat16)


def level_of(rng, dims, cuts, low, top_value):
    def one(position, blocks):
        steps = jax.random.uniform(jax.random.fold_in(jax.random.fold_in(rng, 6), position), (blocks,), jnp.float32, low / len(cuts), top_value / len(cuts))
        return jnp.repeat(jnp.exp(steps), dims[position] // blocks).reshape((-1,) + (1,) * (len(dims) - position - 1))

    factor_of = one(*cuts[0])
    for cut in cuts[1:]:
        factor_of = factor_of * one(*cut)
    return factor_of


def centred(own_key, dims, scale, most, cuts=(), kind=jnp.bfloat16):
    array = jax.random.normal(own_key, dims, jnp.float32) * scale
    if len(cuts) > 0:
        array = level_of(own_key, dims, cuts, -0.22, 0.18) * array
    return jnp.clip(array, min=-most, max=most).astype(kind)


def setup_inputs(seed: int = 0) -> dict:
    key_list = jax.random.split(jax.random.key(seed), 10)
    return {
        "patches": centred(key_list[0], (TOKENS, D), 1.0, 6.0, ((0, 64), (1, 2))),
        "segment": draw_segment(jax.random.fold_in(key_list[9], 71), 0),
        "owner": draw_owner(jax.random.fold_in(key_list[9], 71), 0),
        "w_qkv": draw_w_qkv(jax.random.fold_in(key_list[9], 71), 0),
        "w_out": centred(key_list[4], (D, D), D ** -0.5, 0.15625, ((0, 2),)),
        "w_up": centred(key_list[5], (D, FF), D ** -0.5, 0.15625, ((1, 2),)),
        "w_down": centred(key_list[6], (FF, D), FF ** -0.5, 0.0625, ((0, 2),)),
        "gains": jnp.clip(1.0 + 0.18 * jax.random.normal(key_list[7], (3, D), jnp.float32), 0.1, 1.9),
        "w_merge": centred(key_list[8], (4 * D, OUT), (4 * D) ** -0.5, 0.078125, ((1, 2),)),
    }


def norm_rows(values, gain):
    center = values - lax.optimization_barrier(jnp.mean(values, axis=-1, keepdims=True))
    spread = lax.optimization_barrier(jnp.mean(center * center, axis=-1, keepdims=True))
    return center * lax.rsqrt(spread + 1e-06) * gain

def encode_shard(shard_rows, shard_segment, w_qkv, w_out, w_up, w_down, gains, w_merge):
    count = shard_rows.shape[0]
    resid = shard_rows.astype(jnp.float32)
    normed = norm_rows(resid, gains[0]).astype(jnp.bfloat16)
    query = jnp.dot(normed, w_qkv[0], preferred_element_type=jnp.float32).astype(jnp.bfloat16)
    keys = jnp.dot(normed, w_qkv[1], preferred_element_type=jnp.float32).astype(jnp.bfloat16)
    values = jnp.dot(normed, w_qkv[2], preferred_element_type=jnp.float32).astype(jnp.bfloat16)
    query = query.reshape(count, HEADS, HEAD_DIM).transpose(1, 0, 2)
    keys = keys.reshape(count, HEADS, HEAD_DIM).transpose(1, 0, 2)
    values = values.reshape(count, HEADS, HEAD_DIM).transpose(1, 0, 2)
    same = shard_segment[:, None] == shard_segment[None, :]
    scale = HEAD_DIM ** (-0.5)

    def one_head(operands):
        head_query, head_keys, head_values = operands
        scores = jnp.dot(head_query, head_keys.T, preferred_element_type=jnp.float32) * scale
        scores = jnp.where(same, scores, -1e+30)
        top = lax.optimization_barrier(jnp.max(scores, axis=-1, keepdims=True))
        expo = jnp.exp(scores - top)
        weights = (expo / lax.optimization_barrier(jnp.sum(expo, axis=-1, keepdims=True))).astype(jnp.bfloat16)
        return jnp.dot(weights, head_values, preferred_element_type=jnp.float32).astype(jnp.bfloat16)
    context = lax.map(one_head, (query, keys, values))
    context = context.transpose(1, 0, 2).reshape(count, D)
    resid = resid + jnp.dot(context, w_out, preferred_element_type=jnp.float32)
    normed = norm_rows(resid, gains[1]).astype(jnp.bfloat16)
    hidden = jax.nn.gelu(jnp.dot(normed, w_up, preferred_element_type=jnp.float32), approximate=False).astype(jnp.bfloat16)
    resid = resid + jnp.dot(hidden, w_down, preferred_element_type=jnp.float32)
    final = norm_rows(resid, gains[2]).astype(jnp.bfloat16)
    merged = final.reshape(count // 4, 4 * D)
    return jnp.dot(merged, w_merge, preferred_element_type=jnp.float32).astype(jnp.bfloat16)

def reference(patches, segment, owner, w_qkv, w_out, w_up, w_down, gains, w_merge):
    rows = patches.reshape(N_REQ, TOK_DEV, D)
    segs = segment.reshape(N_REQ, TOK_DEV)

    def per_shard(operands):
        return encode_shard(operands[0], operands[1], w_qkv, w_out, w_up, w_down, gains, w_merge)
    projected = lax.map(per_shard, (rows, segs))
    first_seg = segs[:, ::4]
    owners = owner.reshape(N_REQ, R_DEV)
    picks = first_seg[:, :, None] == jnp.arange(R_DEV, dtype=jnp.int32)[None, None, :]
    looked = lax.optimization_barrier(jnp.sum(jnp.where(picks, owners[:, None, :], 0), axis=2)).astype(jnp.int32)
    dest = jnp.where(first_seg < R_DEV, looked, N_REQ).astype(jnp.int32)
    onehot = (dest[:, :, None] == jnp.arange(N_REQ, dtype=jnp.int32)[None, None, :]).astype(jnp.int32)
    rank = lax.optimization_barrier(jnp.sum((jnp.cumsum(onehot, axis=1) - 1) * onehot, axis=2)).astype(jnp.int32)
    result = jnp.zeros((N_REQ, R_DEV, CAP, OUT), jnp.bfloat16)
    result = result.at[dest.reshape(-1), first_seg.reshape(-1), rank.reshape(-1)].set(projected.reshape(-1, OUT), mode='drop')
    return result.reshape(N_REQ * R_DEV * CAP, OUT)
```

```python
import functools

import jax
import jax.numpy as jnp
from jax import lax
from jax.experimental import pallas as pl
from jax.experimental.pallas import tpu as pltpu
from jax.sharding import PartitionSpec as P

HEAD_DIM = 104
CAP = 32
MESH = pl.DeviceIdType.MESH


def norm_rows(values, gain):
    center = values - jnp.mean(values, axis=-1, keepdims=True)
    spread = jnp.mean(center * center, axis=-1, keepdims=True)
    return center * lax.rsqrt(spread + 1e-06) * gain


def attend(query, keys, values, segment):
    count = query.shape[0]
    scale = HEAD_DIM ** (-0.5)
    scores = jnp.einsum("qhd,khd->hqk", query, keys, preferred_element_type=jnp.float32) * scale
    same = segment[:, None] == segment[None, :]
    scores = jnp.where(same[None], scores, -1e30)
    top = jnp.max(scores, axis=-1, keepdims=True)
    expo = jnp.exp(scores - top)
    weights = (expo / jnp.sum(expo, axis=-1, keepdims=True)).astype(jnp.bfloat16)
    context = jnp.einsum(
        "hqk,khd->qhd", weights, values, preferred_element_type=jnp.float32
    ).astype(jnp.bfloat16)
    return context.reshape(count, -1)


def peer_of(me, step):
    x = lax.rem(lax.rem(me, 4) + lax.rem(step, 4) + 2, 4)
    y = lax.rem(lax.rem(me // 4, 4) + lax.rem(step // 4, 4) + 2, 4)
    z = lax.rem(me // 16 + step // 16 + 2, 4)
    return (z * 4 + y) * 4 + x


SELF_STEP = 42


def route_kernel(
    merged_ref, weight_ref, owner_ref, out_ref,
    wbuf, acc, tiles, inbox, sorted_tiles, landed, own_rows, table, inv_v, inv_s,
    w_sems, send_sem1, recv_sem1, send_sem2, recv_sem2, send_semo, recv_semo, inv_sem,
):
    chunks, depth = wbuf.shape[0], wbuf.shape[1]
    me = lax.axis_index("req")

    def weight_copy(k):
        return pltpu.make_async_copy(weight_ref.at[pl.ds(k * depth, depth), :], wbuf.at[k], w_sems.at[k])

    @pl.loop(0, chunks)
    def _(k):
        weight_copy(k).start()

    barrier = pltpu.get_barrier_semaphore()

    @pl.loop(0, 64)
    def _(step):
        @pl.when(step != SELF_STEP)
        def _():
            pl.semaphore_signal(barrier, inc=1, device_id={"req": peer_of(me, step)}, device_id_type=MESH)

    for j in range(2):
        own_rows[j] = jnp.full((1, 128), owner_ref[j], jnp.int32)

    acc[...] = jnp.zeros_like(acc)

    def step_matmul(k):
        weight_copy(k).wait()
        lhs = merged_ref[:, pl.ds(pl.multiple_of(k * depth, depth), depth)]
        acc[...] += jnp.dot(lhs, wbuf[k], preferred_element_type=jnp.float32)

    first = chunks - 3

    @pl.loop(0, first)
    def _(k):
        step_matmul(k)

    pl.semaphore_wait(barrier, 63)

    @pl.loop(0, 64)
    def _(step):
        @pl.when(step != SELF_STEP)
        def _():
            peer = peer_of(me, step)
            pltpu.make_async_remote_copy(
                src_ref=own_rows.at[peer // 32], dst_ref=table.at[me], send_sem=send_semo, recv_sem=recv_semo,
                device_id={"req": peer}, device_id_type=MESH,
            ).start()

    @pl.loop(first, chunks)
    def _(k):
        step_matmul(k)

    for g in range(4):
        for c in range(16):
            tiles[g * 16 + c] = acc[pl.ds(16 * g, 16), pl.ds(128 * c, 128)].astype(jnp.bfloat16)

    @pl.loop(0, 64)
    def _(step):
        @pl.when(step != SELF_STEP)
        def _():
            peer = peer_of(me, step)
            pltpu.make_async_remote_copy(
                src_ref=tiles.at[peer], dst_ref=inbox.at[me], send_sem=send_sem1, recv_sem=recv_sem1,
                device_id={"req": peer}, device_id_type=MESH,
            ).start()

    inbox[me] = tiles[me]
    table[me] = own_rows[me // 32]

    pltpu.make_async_copy(table.at[pl.ds(0, 63)], table.at[pl.ds(0, 63)], recv_semo).wait()
    lanes = lax.broadcasted_iota(jnp.int32, (64, 1, 128), 2)
    sources = lax.broadcasted_iota(jnp.int32, (64, 1, 128), 0)
    inv_v[...] = jnp.max(jnp.where(table[...] == lanes, sources, 0), axis=0)
    to_scalar = pltpu.make_async_copy(inv_v, inv_s, inv_sem)
    to_scalar.start()
    to_scalar.wait()

    pltpu.make_async_copy(inbox.at[pl.ds(0, 63)], inbox.at[pl.ds(0, 63)], recv_sem1).wait()

    @pl.loop(0, 64)
    def _(d):
        sorted_tiles[d] = inbox[inv_s[0, d]]

    @pl.loop(0, 64)
    def _(step):
        @pl.when(step != SELF_STEP)
        def _():
            peer = peer_of(me, step)
            pltpu.make_async_remote_copy(
                src_ref=sorted_tiles.at[peer], dst_ref=landed.at[me], send_sem=send_sem2, recv_sem=recv_sem2,
                device_id={"req": peer}, device_id_type=MESH,
            ).start()

    landed[me] = sorted_tiles[me]
    pltpu.make_async_copy(landed.at[pl.ds(0, 63)], landed.at[pl.ds(0, 63)], recv_sem2).wait()
    for g in range(4):
        for c in range(16):
            out_ref[pl.ds(16 * g, 16), pl.ds(128 * c, 128)] = landed[g * 16 + c]
    pltpu.make_async_copy(table.at[pl.ds(0, 63)], table.at[pl.ds(0, 63)], send_semo).wait()
    pltpu.make_async_copy(tiles.at[pl.ds(0, 63)], tiles.at[pl.ds(0, 63)], send_sem1).wait()
    pltpu.make_async_copy(sorted_tiles.at[pl.ds(0, 63)], sorted_tiles.at[pl.ds(0, 63)], send_sem2).wait()


def route(merged, w_merge, owner):
    rows, depth = merged.shape
    width = w_merge.shape[1]
    chunk = 512
    chunks = depth // chunk
    return pl.pallas_call(
        route_kernel,
        out_shape=jax.ShapeDtypeStruct((rows, width), jnp.bfloat16),
        in_specs=[
            pl.BlockSpec(memory_space=pltpu.VMEM),
            pl.BlockSpec(memory_space=pl.ANY),
            pl.BlockSpec(memory_space=pltpu.SMEM),
        ],
        out_specs=pl.BlockSpec(memory_space=pltpu.VMEM),
        scratch_shapes=[
            pltpu.VMEM((chunks, chunk, width), jnp.bfloat16),
            pltpu.VMEM((rows, width), jnp.float32),
            pltpu.VMEM((64, 16, 128), jnp.bfloat16),
            pltpu.VMEM((64, 16, 128), jnp.bfloat16),
            pltpu.VMEM((64, 16, 128), jnp.bfloat16),
            pltpu.VMEM((64, 16, 128), jnp.bfloat16),
            pltpu.VMEM((2, 1, 128), jnp.int32),
            pltpu.VMEM((64, 1, 128), jnp.int32),
            pltpu.VMEM((1, 128), jnp.int32),
            pltpu.SMEM((1, 128), jnp.int32),
            pltpu.SemaphoreType.DMA((chunks,)),
        ]
        + [pltpu.SemaphoreType.DMA] * 7,
        compiler_params=pltpu.CompilerParams(
            collective_id=1, has_side_effects=True, vmem_limit_bytes=48 * 1024 * 1024
        ),
        name="route",
    )(merged, w_merge, owner)


def local(patches, segment, owner, w_qkv, w_out, w_up, w_down, gains, w_merge):
    rows_full = lax.all_gather(patches, "tp", axis=1, tiled=True)
    count = rows_full.shape[0]
    width = rows_full.shape[1]
    resid = rows_full.astype(jnp.float32)
    normed = norm_rows(resid, gains[0]).astype(jnp.bfloat16)
    packed = jnp.einsum("td,sde->ste", normed, w_qkv, preferred_element_type=jnp.float32).astype(
        jnp.bfloat16
    )
    local_heads = w_qkv.shape[2] // HEAD_DIM
    query = packed[0].reshape(count, local_heads, HEAD_DIM)
    keys = packed[1].reshape(count, local_heads, HEAD_DIM)
    values = packed[2].reshape(count, local_heads, HEAD_DIM)
    context = attend(query, keys, values, segment)
    first = resid + lax.psum(
        jnp.dot(context, w_out, preferred_element_type=jnp.float32).astype(jnp.bfloat16), "tp"
    ).astype(jnp.float32)
    hidden = jax.nn.gelu(
        jnp.dot(
            norm_rows(first, gains[1]).astype(jnp.bfloat16),
            w_up,
            preferred_element_type=jnp.float32,
        ),
        approximate=False,
    ).astype(jnp.bfloat16)
    second = first + lax.psum(
        jnp.dot(hidden, w_down, preferred_element_type=jnp.float32).astype(jnp.bfloat16), "tp"
    ).astype(jnp.float32)
    final = norm_rows(second, gains[2]).astype(jnp.bfloat16)
    first_seg = segment[::4]
    index = jnp.arange(count // 4, dtype=jnp.int32)
    starts = jnp.sum((first_seg[None, :] < jnp.arange(2, dtype=jnp.int32)[:, None]).astype(jnp.int32), axis=1)
    want = (starts[:, None] + jnp.arange(CAP, dtype=jnp.int32)[None, :]).reshape(-1)
    request = jnp.repeat(jnp.arange(2, dtype=jnp.int32), CAP)
    pick = ((want[:, None] == index[None, :]) & (first_seg[None, :] == request[:, None])).astype(jnp.bfloat16)
    merged = jnp.dot(
        pick, final.reshape(count // 4, 4 * width), preferred_element_type=jnp.float32
    ).astype(jnp.bfloat16)
    return route(merged, w_merge, owner)


def solution(mesh):
    in_specs = (
        P("req", "tp"),
        P("req"),
        P("req"),
        P(None, None, "tp"),
        P("tp", None),
        P(None, "tp"),
        P("tp", None),
        P(),
        P(None, "tp"),
    )
    out_specs = P("req", "tp")
    return jax.shard_map(local, mesh=mesh, in_specs=in_specs, out_specs=out_specs, check_vma=False)
```

```python
import functools

import jax
import jax.numpy as jnp
from jax import lax
from jax.experimental import pallas as pl
from jax.experimental.pallas import tpu as pltpu
from jax.sharding import PartitionSpec as P

HEAD_DIM = 104
CAP = 32
MESH = pl.DeviceIdType.MESH


def peer_of(me, step):
    x = lax.rem(lax.rem(me, 4) + lax.rem(step, 4) + 2, 4)
    y = lax.rem(lax.rem(me // 4, 4) + lax.rem(step // 4, 4) + 2, 4)
    z = lax.rem(me // 16 + step // 16 + 2, 4)
    return (z * 4 + y) * 4 + x


SELF_STEP = 42


def route_kernel(
    merged_ref, weight_ref, owner_ref, out_ref,
    wbuf, acc, tiles, inbox, sorted_tiles, landed, own_rows, table, inv_v, inv_s,
    w_sems, send_sem1, recv_sem1, send_sem2, recv_sem2, send_semo, recv_semo, inv_sem,
):
    chunks, depth = wbuf.shape[0], wbuf.shape[1]
    me = lax.axis_index("req")

    def weight_copy(k):
        return pltpu.make_async_copy(weight_ref.at[pl.ds(k * depth, depth), :], wbuf.at[k], w_sems.at[k])

    @pl.loop(0, chunks)
    def _(k):
        weight_copy(k).start()

    barrier = pltpu.get_barrier_semaphore()

    @pl.loop(0, 64)
    def _(step):
        @pl.when(step != SELF_STEP)
        def _():
            pl.semaphore_signal(barrier, inc=1, device_id={"req": peer_of(me, step)}, device_id_type=MESH)

    for j in range(2):
        own_rows[j] = jnp.full((1, 128), owner_ref[j], jnp.int32)

    acc[...] = jnp.zeros_like(acc)

    def step_matmul(k):
        weight_copy(k).wait()
        lhs = merged_ref[:, pl.ds(pl.multiple_of(k * depth, depth), depth)]
        acc[...] += jnp.dot(lhs, wbuf[k], preferred_element_type=jnp.float32)

    first = chunks - 3

    @pl.loop(0, first)
    def _(k):
        step_matmul(k)

    pl.semaphore_wait(barrier, 63)

    @pl.loop(0, 64)
    def _(step):
        @pl.when(step != SELF_STEP)
        def _():
            peer = peer_of(me, step)
            pltpu.make_async_remote_copy(
                src_ref=own_rows.at[peer // 32], dst_ref=table.at[me], send_sem=send_semo, recv_sem=recv_semo,
                device_id={"req": peer}, device_id_type=MESH,
            ).start()

    @pl.loop(first, chunks)
    def _(k):
        step_matmul(k)

    for g in range(4):
        for c in range(16):
            tiles[g * 16 + c] = acc[pl.ds(16 * g, 16), pl.ds(128 * c, 128)].astype(jnp.bfloat16)

    @pl.loop(0, 64)
    def _(step):
        @pl.when(step != SELF_STEP)
        def _():
            peer = peer_of(me, step)
            pltpu.make_async_remote_copy(
                src_ref=tiles.at[peer], dst_ref=inbox.at[me], send_sem=send_sem1, recv_sem=recv_sem1,
                device_id={"req": peer}, device_id_type=MESH,
            ).start()

    inbox[me] = tiles[me]
    table[me] = own_rows[me // 32]

    pltpu.make_async_copy(table.at[pl.ds(0, 63)], table.at[pl.ds(0, 63)], recv_semo).wait()
    lanes = lax.broadcasted_iota(jnp.int32, (64, 1, 128), 2)
    sources = lax.broadcasted_iota(jnp.int32, (64, 1, 128), 0)
    inv_v[...] = jnp.max(jnp.where(table[...] == lanes, sources, 0), axis=0)
    to_scalar = pltpu.make_async_copy(inv_v, inv_s, inv_sem)
    to_scalar.start()
    to_scalar.wait()

    pltpu.make_async_copy(inbox.at[pl.ds(0, 63)], inbox.at[pl.ds(0, 63)], recv_sem1).wait()

    @pl.loop(0, 64)
    def _(d):
        sorted_tiles[d] = inbox[inv_s[0, d]]

    @pl.loop(0, 64)
    def _(step):
        @pl.when(step != SELF_STEP)
        def _():
            peer = peer_of(me, step)
            pltpu.make_async_remote_copy(
                src_ref=sorted_tiles.at[peer], dst_ref=landed.at[me], send_sem=send_sem2, recv_sem=recv_sem2,
                device_id={"req": peer}, device_id_type=MESH,
            ).start()

    landed[me] = sorted_tiles[me]
    pltpu.make_async_copy(landed.at[pl.ds(0, 63)], landed.at[pl.ds(0, 63)], recv_sem2).wait()
    for g in range(4):
        for c in range(16):
            out_ref[pl.ds(16 * g, 16), pl.ds(128 * c, 128)] = landed[g * 16 + c]
    pltpu.make_async_copy(table.at[pl.ds(0, 63)], table.at[pl.ds(0, 63)], send_semo).wait()
    pltpu.make_async_copy(tiles.at[pl.ds(0, 63)], tiles.at[pl.ds(0, 63)], send_sem1).wait()
    pltpu.make_async_copy(sorted_tiles.at[pl.ds(0, 63)], sorted_tiles.at[pl.ds(0, 63)], send_sem2).wait()


def route(merged, w_merge, owner):
    rows, depth = merged.shape
    width = w_merge.shape[1]
    chunk = 512
    chunks = depth // chunk
    return pl.pallas_call(
        route_kernel,
        out_shape=jax.ShapeDtypeStruct((rows, width), jnp.bfloat16),
        in_specs=[
            pl.BlockSpec(memory_space=pltpu.VMEM),
            pl.BlockSpec(memory_space=pl.ANY),
            pl.BlockSpec(memory_space=pltpu.SMEM),
        ],
        out_specs=pl.BlockSpec(memory_space=pltpu.VMEM),
        scratch_shapes=[
            pltpu.VMEM((chunks, chunk, width), jnp.bfloat16),
            pltpu.VMEM((rows, width), jnp.float32),
            pltpu.VMEM((64, 16, 128), jnp.bfloat16),
            pltpu.VMEM((64, 16, 128), jnp.bfloat16),
            pltpu.VMEM((64, 16, 128), jnp.bfloat16),
            pltpu.VMEM((64, 16, 128), jnp.bfloat16),
            pltpu.VMEM((2, 1, 128), jnp.int32),
            pltpu.VMEM((64, 1, 128), jnp.int32),
            pltpu.VMEM((1, 128), jnp.int32),
            pltpu.SMEM((1, 128), jnp.int32),
            pltpu.SemaphoreType.DMA((chunks,)),
        ]
        + [pltpu.SemaphoreType.DMA] * 7,
        compiler_params=pltpu.CompilerParams(
            collective_id=1, has_side_effects=True, vmem_limit_bytes=48 * 1024 * 1024
        ),
        name="route",
    )(merged, w_merge, owner)


def encode_kernel(
    patches_ref, segment_ref, qkv_ref, wout_ref, up_ref, down_ref, gains_ref, merged_ref,
    x_t, qkv_buf, wout_buf, up_buf, down_buf, normed_t, heads, context, resid, acc, normed,
    pre_a, pre_b, hid_a, hid_b, sent1, got1, sent2, got2,
    x_sem, qkv_sems, wout_sems, up_sems, down_sems, xs_sem, xr_sem, s1_sems, r1_sems, s2_sems, r2_sems,
):
    f32, bf16 = jnp.float32, jnp.bfloat16
    tp = lax.axis_index("tp")
    partner = {"tp": 1 - tp}
    half = patches_ref.shape[0]
    count = patches_ref.shape[1]
    width = 2 * half
    head_count = half // HEAD_DIM
    hidden_chunk = up_buf.shape[2]
    hidden_chunks = up_buf.shape[0]
    cuts = [(0, 512), (512, 512), (1024, 640)]

    def x_copy():
        return pltpu.make_async_copy(patches_ref, x_t.at[pl.ds(tp * half, half), :], x_sem)

    def qkv_copy(s):
        return pltpu.make_async_copy(qkv_ref.at[s], qkv_buf.at[s], qkv_sems.at[s])

    def wout_copy(h):
        return pltpu.make_async_copy(
            wout_ref.at[pl.ds(HEAD_DIM * h, HEAD_DIM), :], wout_buf.at[pl.ds(128 * h, HEAD_DIM), :], wout_sems.at[h]
        )

    def up_copy(c):
        return pltpu.make_async_copy(
            up_ref.at[:, pl.ds(hidden_chunk * c, hidden_chunk)], up_buf.at[c], up_sems.at[c]
        )

    def down_copy(c):
        return pltpu.make_async_copy(
            down_ref.at[pl.ds(hidden_chunk * c, hidden_chunk), :], down_buf.at[c], down_sems.at[c]
        )

    def remote(src, dst, send, recv):
        return pltpu.make_async_remote_copy(
            src_ref=src, dst_ref=dst, send_sem=send, recv_sem=recv, device_id=partner, device_id_type=MESH
        )

    x_copy().start()
    for s in range(3):
        qkv_copy(s).start()

    barrier = pltpu.get_barrier_semaphore()
    pl.semaphore_signal(barrier, inc=1, device_id=partner, device_id_type=MESH)
    pl.semaphore_wait(barrier, 1)
    x_swap = remote(patches_ref, x_t.at[pl.ds(tp * half, half), :], xs_sem, xr_sem)
    x_swap.start()

    for h in range(head_count):
        wout_buf[pl.ds(128 * h + HEAD_DIM, 128 - HEAD_DIM), :] = jnp.zeros((128 - HEAD_DIM, width), bf16)
        for s in range(3):
            heads[s, h, pl.ds(HEAD_DIM, 128 - HEAD_DIM), :] = jnp.zeros((128 - HEAD_DIM, count), bf16)
    seg_rows = jnp.broadcast_to(segment_ref[...], (count, count))
    same = seg_rows == seg_rows.T

    x_copy().wait()
    x_swap.wait()

    total = jnp.zeros((1, count), f32)
    for b in range(width // 128):
        total += jnp.sum(x_t[pl.ds(128 * b, 128), :].astype(f32), axis=0, keepdims=True)
    mean = total * (1.0 / width)
    total = jnp.zeros((1, count), f32)
    for b in range(width // 128):
        center = x_t[pl.ds(128 * b, 128), :].astype(f32) - mean
        total += jnp.sum(center * center, axis=0, keepdims=True)
    scale = lax.rsqrt(total * (1.0 / width) + 1e-06)
    for b in range(width // 128):
        gain = jnp.broadcast_to(gains_ref[0:1, pl.ds(128 * b, 128)], (128, 128)).T
        gain = jnp.concatenate([gain] * (count // 128), axis=1)
        x = x_t[pl.ds(128 * b, 128), :].astype(f32)
        normed_t[pl.ds(128 * b, 128), :] = ((x - mean) * scale * gain).astype(bf16)
        resid[:, pl.ds(128 * b, 128)] = x.T

    for s in range(3):
        qkv_copy(s).wait()
        if s == 0:
            for h in range(head_count):
                wout_copy(h).start()
        for c in range(s * 3, min(s * 3 + 3, hidden_chunks)):
            up_copy(c).start()
            down_copy(c).start()
        product = jnp.dot(qkv_buf[s], normed_t[...], preferred_element_type=f32)
        for h in range(head_count):
            heads[s, h, pl.ds(0, HEAD_DIM), :] = product[HEAD_DIM * h : HEAD_DIM * (h + 1)].astype(bf16)

    for h in range(head_count):
        scores = lax.dot_general(
            heads[1, h], heads[0, h], (((0,), (0,)), ((), ())), preferred_element_type=f32
        )
        scores = jnp.where(same, scores * HEAD_DIM ** (-0.5), -1e30)
        top = jnp.max(scores, axis=0, keepdims=True)
        expo = jnp.exp(scores - top)
        share = 1.0 / jnp.sum(expo, axis=0, keepdims=True)
        mixed = jnp.dot(heads[2, h], expo.astype(bf16), preferred_element_type=f32) * share
        context[:, pl.ds(128 * h, 128)] = mixed.T.astype(bf16)

    for h in range(head_count):
        wout_copy(h).wait()
    swaps = []
    for k, (start, size) in enumerate(cuts):
        cols = pl.ds(start, size)
        product = jnp.dot(context[...], wout_buf[:, cols], preferred_element_type=f32)
        sent1[:, cols] = product.astype(bf16)
        swap = remote(sent1.at[:, cols], got1.at[:, cols], s1_sems.at[k], r1_sems.at[k])
        swap.start()
        swaps.append(swap)
        resid[:, cols] += product

    for swap in swaps:
        swap.wait()

    def norm_to(which, out, extra):
        for b in range(count // 32):
            rows = pl.ds(32 * b, 32)
            x = resid[rows, :] + extra[rows, :].astype(f32)
            resid[rows, :] = x
            center = x - jnp.sum(x, axis=1, keepdims=True) * (1.0 / width)
            spread = jnp.sum(center * center, axis=1, keepdims=True) * (1.0 / width)
            out[rows, :] = (center * lax.rsqrt(spread + 1e-06) * gains_ref[which : which + 1, :]).astype(bf16)

    norm_to(1, normed, got1)

    def up(c, out):
        up_copy(c).wait()
        out[...] = jnp.dot(normed[...], up_buf[c], preferred_element_type=f32)

    def gelu(pre, out):
        u = pre[...]
        out[...] = (0.5 * u * (1.0 + lax.erf(u * 0.5**0.5))).astype(bf16)

    def down(c, hid):
        down_copy(c).wait()
        acc[...] += jnp.dot(hid[...], down_buf[c], preferred_element_type=f32)

    acc[...] = jnp.zeros_like(acc)
    up(0, pre_a)
    up(1, pre_b)
    gelu(pre_a, hid_a)

    @pl.loop(0, hidden_chunks // 2 - 1)
    def _(i):
        c = 2 * i
        up(c + 2, pre_a)
        gelu(pre_b, hid_b)
        down(c, hid_a)
        up(c + 3, pre_b)
        gelu(pre_a, hid_a)
        down(c + 1, hid_b)

    gelu(pre_b, hid_b)
    down(hidden_chunks - 2, hid_a)
    down_copy(hidden_chunks - 1).wait()
    swaps = []
    for k, (start, size) in enumerate(cuts):
        cols = pl.ds(start, size)
        product = acc[:, cols] + jnp.dot(
            hid_b[...], down_buf[hidden_chunks - 1, :, cols], preferred_element_type=f32
        )
        sent2[:, cols] = product.astype(bf16)
        swap = remote(sent2.at[:, cols], got2.at[:, cols], s2_sems.at[k], r2_sems.at[k])
        swap.start()
        swaps.append(swap)
        resid[:, cols] += product

    row = lax.broadcasted_iota(jnp.int32, (count, count), 0)
    token = lax.broadcasted_iota(jnp.int32, (count, count), 1)
    quarter = count // 4
    part, request, rank = row // quarter, lax.rem(row, quarter) // CAP, lax.rem(row, CAP)
    first = jnp.sum((segment_ref[...] < 1).astype(jnp.int32), axis=1, keepdims=True)
    want = request * first + 4 * rank + part
    pick = jnp.where((token == want) & (segment_ref[...] == request), 1.0, 0.0).astype(bf16)

    for swap in swaps:
        swap.wait()
    norm_to(2, normed, got2)
    for i in range(4):
        merged_ref[:, pl.ds(width * i, width)] = jnp.dot(
            pick[quarter * i : quarter * (i + 1)], normed[...], preferred_element_type=f32
        ).astype(bf16)


def encode(patches_t, segment, qkv_t, w_out, w_up, w_down, gains):
    half, count = patches_t.shape
    width = 2 * half
    hidden = w_up.shape[1]
    chunk = 512
    chunks = hidden // chunk
    heads = half // HEAD_DIM
    f32, bf16 = jnp.float32, jnp.bfloat16
    vmem = pl.BlockSpec(memory_space=pltpu.VMEM)
    anywhere = pl.BlockSpec(memory_space=pl.ANY)
    dma = pltpu.SemaphoreType.DMA
    return pl.pallas_call(
        encode_kernel,
        out_shape=jax.ShapeDtypeStruct((count // 4, 4 * width), bf16),
        in_specs=[anywhere, vmem, anywhere, anywhere, anywhere, anywhere, vmem],
        out_specs=vmem,
        scratch_shapes=[
            pltpu.VMEM((width, count), bf16),
            pltpu.VMEM((3, half, width), bf16),
            pltpu.VMEM((heads * 128, width), bf16),
            pltpu.VMEM((chunks, width, chunk), bf16),
            pltpu.VMEM((chunks, chunk, width), bf16),
            pltpu.VMEM((width, count), bf16),
            pltpu.VMEM((3, heads, 128, count), bf16),
            pltpu.VMEM((count, heads * 128), bf16),
            pltpu.VMEM((count, width), f32),
            pltpu.VMEM((count, width), f32),
            pltpu.VMEM((count, width), bf16),
            pltpu.VMEM((count, chunk), f32),
            pltpu.VMEM((count, chunk), f32),
            pltpu.VMEM((count, chunk), bf16),
            pltpu.VMEM((count, chunk), bf16),
        ]
        + [pltpu.VMEM((count, width), bf16)] * 4
        + [dma, dma((3,)), dma((heads,)), dma((chunks,)), dma((chunks,)), dma, dma]
        + [dma((3,))] * 4,
        compiler_params=pltpu.CompilerParams(
            collective_id=2, has_side_effects=True, vmem_limit_bytes=60 * 1024 * 1024
        ),
        name="encode",
    )(patches_t, segment, qkv_t, w_out, w_up, w_down, gains)


def local(patches, segment, owner, w_qkv, w_out, w_up, w_down, gains, w_merge):
    merged = encode(
        patches.T, segment.reshape(1, -1), w_qkv.transpose(0, 2, 1), w_out, w_up, w_down, gains
    )
    return route(merged, w_merge, owner)


def solution(mesh):
    in_specs = (
        P("req", "tp"),
        P("req"),
        P("req"),
        P(None, None, "tp"),
        P("tp", None),
        P(None, "tp"),
        P("tp", None),
        P(),
        P(None, "tp"),
    )
    out_specs = P("req", "tp")
    return jax.shard_map(local, mesh=mesh, in_specs=in_specs, out_specs=out_specs, check_vma=False)
```

```python
import functools

import jax
import jax.numpy as jnp
from jax import lax
from jax.experimental import pallas as pl
from jax.experimental.pallas import tpu as pltpu
from jax.sharding import PartitionSpec as P

HEAD_DIM = 104
CAP = 32
MESH = pl.DeviceIdType.MESH


class Place:
    def __init__(self):
        self.me = lax.axis_index("req")
        x, y, z = lax.rem(self.me, 4), lax.rem(self.me // 4, 4), self.me // 16
        self.x = [lax.rem(x + k, 4) for k in range(4)]
        self.y = [lax.rem(y + k, 4) for k in range(4)]
        self.z = [lax.rem(z + k, 4) for k in range(4)]

    def peer(self, dz, dy, dx):
        return self.z[dz] * 16 + self.y[dy] * 4 + self.x[dx]

    def others(self, dys=(2, 3, 1, 0)):
        for dy in dys:
            for dz in (2, 3, 1, 0):
                for dx in (2, 3, 1, 0):
                    if (dz, dy, dx) != (0, 0, 0):
                        yield self.peer(dz, dy, dx)


def swap_kernel(patches_ref, out_ref, x_sem, send_sem, recv_sem):
    tp = lax.axis_index("tp")
    half = patches_ref.shape[0]
    place = out_ref.at[pl.ds(tp * half, half), :]
    mine = pltpu.make_async_copy(patches_ref, place, x_sem)
    mine.start()
    barrier = pltpu.get_barrier_semaphore()
    pl.semaphore_signal(barrier, inc=1, device_id={"tp": 1 - tp}, device_id_type=MESH)
    pl.semaphore_wait(barrier, 1)
    swap = pltpu.make_async_remote_copy(
        src_ref=patches_ref, dst_ref=place, send_sem=send_sem, recv_sem=recv_sem,
        device_id={"tp": 1 - tp}, device_id_type=MESH,
    )
    swap.start()
    mine.wait()
    swap.wait()


def swap_halves(patches_t):
    half, count = patches_t.shape
    dma = pltpu.SemaphoreType.DMA
    return pl.pallas_call(
        swap_kernel,
        out_shape=jax.ShapeDtypeStruct((2 * half, count), patches_t.dtype),
        in_specs=[pl.BlockSpec(memory_space=pl.ANY)],
        out_specs=pl.BlockSpec(memory_space=pltpu.VMEM),
        scratch_shapes=[dma, dma, dma],
        compiler_params=pltpu.CompilerParams(
            collective_id=1, has_side_effects=True, vmem_limit_bytes=62 * 1024 * 1024
        ),
        name="swap_halves",
    )(patches_t)


def layer_kernel(
    x_ref, segment_ref, owner_ref, qkv_ref, wout_ref, up_ref, down_ref, gains_ref, merge_ref, out_ref,
    x_t, qkv_buf, wout_buf, pool, down_buf, normed_t, heads, context, resid, acc, normed,
    pre_a, pre_b, hid_a, hid_b, sent1, got1, sent2, got2,
    merged, tiles, inbox, sorted_tiles, landed, own_rows, table, inv_v, inv_s,
    x_sem, qkv_sems, wout_sems, pool_sems, down_sems, s1_sems, r1_sems, s2_sems, r2_sems,
    send_sem_o, recv_sem_o, inv_sem, send_sem_a, recv_sem_a, send_sem_b, recv_sem_b,
):
    f32, bf16 = jnp.float32, jnp.bfloat16
    tp = lax.axis_index("tp")
    partner = {"tp": 1 - tp}
    place = Place()
    me = place.me
    width, count = x_t.shape
    half = width // 2
    head_count = half // HEAD_DIM
    slots, _, hidden_chunk = pool.shape
    hidden_chunks = down_buf.shape[0]
    out_chunks = merge_ref.shape[1] // hidden_chunk
    cuts = [(0, 512), (512, 512), (1024, 640)]

    def qkv_copy(s):
        return pltpu.make_async_copy(qkv_ref.at[s], qkv_buf.at[s], qkv_sems.at[s])

    def wout_copy(h):
        return pltpu.make_async_copy(
            wout_ref.at[pl.ds(HEAD_DIM * h, HEAD_DIM), :], wout_buf.at[pl.ds(128 * h, HEAD_DIM), :], wout_sems.at[h]
        )

    def up_copy(c):
        return pltpu.make_async_copy(
            up_ref.at[:, pl.ds(hidden_chunk * c, hidden_chunk)], pool.at[c], pool_sems.at[c]
        )

    def merge_cols(m):
        return pl.ds(pl.multiple_of(place.y[(2, 3, 1, 0)[m // 4]] * hidden_chunk, hidden_chunk), hidden_chunk)

    def merge_copy(m):
        slot = (hidden_chunks + m) % slots
        return pltpu.make_async_copy(
            merge_ref.at[pl.ds(width * (m % 4), width), merge_cols(m)], pool.at[slot], pool_sems.at[slot]
        )

    def down_copy(c):
        return pltpu.make_async_copy(
            down_ref.at[pl.ds(hidden_chunk * c, hidden_chunk), :], down_buf.at[c], down_sems.at[c]
        )

    def remote(src, dst, send, recv):
        return pltpu.make_async_remote_copy(
            src_ref=src, dst_ref=dst, send_sem=send, recv_sem=recv, device_id=partner, device_id_type=MESH
        )

    x_copy = pltpu.make_async_copy(x_ref, x_t, x_sem)
    x_copy.start()
    for s in range(3):
        qkv_copy(s).start()

    barrier = pltpu.get_barrier_semaphore()
    for peer in place.others():
        pl.semaphore_signal(barrier, inc=1, device_id={"req": peer}, device_id_type=MESH)
    pl.semaphore_signal(barrier, inc=1, device_id=partner, device_id_type=MESH)

    for j in range(2):
        own_rows[j] = jnp.full((1, 128), owner_ref[j], jnp.int32)
    for h in range(head_count):
        wout_buf[pl.ds(128 * h + HEAD_DIM, 128 - HEAD_DIM), :] = jnp.zeros((128 - HEAD_DIM, width), bf16)
        for s in range(3):
            heads[s, h, pl.ds(HEAD_DIM, 128 - HEAD_DIM), :] = jnp.zeros((128 - HEAD_DIM, count), bf16)
    seg_rows = jnp.broadcast_to(segment_ref[...], (count, count))
    same = seg_rows == seg_rows.T

    x_copy.wait()
    total = jnp.zeros((1, count), f32)
    for b in range(width // 128):
        total += jnp.sum(x_t[pl.ds(128 * b, 128), :].astype(f32), axis=0, keepdims=True)
    mean = total * (1.0 / width)
    total = jnp.zeros((1, count), f32)
    for b in range(width // 128):
        center = x_t[pl.ds(128 * b, 128), :].astype(f32) - mean
        total += jnp.sum(center * center, axis=0, keepdims=True)
    scale = lax.rsqrt(total * (1.0 / width) + 1e-06)
    for b in range(width // 128):
        gain = jnp.broadcast_to(gains_ref[0:1, pl.ds(128 * b, 128)], (128, 128)).T
        gain = jnp.concatenate([gain] * (count // 128), axis=1)
        x = x_t[pl.ds(128 * b, 128), :].astype(f32)
        normed_t[pl.ds(128 * b, 128), :] = ((x - mean) * scale * gain).astype(bf16)
        resid[:, pl.ds(128 * b, 128)] = x.T

    for s in range(3):
        qkv_copy(s).wait()
        if s == 0:
            for h in range(head_count):
                wout_copy(h).start()
        for c in range(s * 3, min(s * 3 + 3, hidden_chunks)):
            up_copy(c).start()
            down_copy(c).start()
        if s == 2:
            for m in range(slots - hidden_chunks):
                merge_copy(m).start()
        product = jnp.dot(qkv_buf[s], normed_t[...], preferred_element_type=f32)
        for h in range(head_count):
            heads[s, h, pl.ds(0, HEAD_DIM), :] = product[HEAD_DIM * h : HEAD_DIM * (h + 1)].astype(bf16)

    for h in range(head_count):
        scores = lax.dot_general(
            heads[1, h], heads[0, h], (((0,), (0,)), ((), ())), preferred_element_type=f32
        )
        scores = jnp.where(same, scores * HEAD_DIM ** (-0.5), -1e30)
        top = jnp.max(scores, axis=0, keepdims=True)
        expo = jnp.exp(scores - top)
        share = 1.0 / jnp.sum(expo, axis=0, keepdims=True)
        mixed = jnp.dot(heads[2, h], expo.astype(bf16), preferred_element_type=f32) * share
        context[:, pl.ds(128 * h, 128)] = mixed.T.astype(bf16)

    for h in range(head_count):
        wout_copy(h).wait()
    pl.semaphore_wait(barrier, 64)
    swaps = []
    for k, (start, size) in enumerate(cuts):
        cols = pl.ds(start, size)
        product = jnp.dot(context[...], wout_buf[:, cols], preferred_element_type=f32)
        sent1[:, cols] = product.astype(bf16)
        swap = remote(sent1.at[:, cols], got1.at[:, cols], s1_sems.at[k], r1_sems.at[k])
        swap.start()
        swaps.append(swap)
        resid[:, cols] += product

    for peer in place.others():
        pltpu.make_async_remote_copy(
            src_ref=own_rows.at[peer // 32], dst_ref=table.at[me], send_sem=send_sem_o, recv_sem=recv_sem_o,
            device_id={"req": peer}, device_id_type=MESH,
        ).start()
    table[me] = own_rows[me // 32]

    for swap in swaps:
        swap.wait()

    def norm_to(which, out, extra):
        for b in range(count // 32):
            rows = pl.ds(32 * b, 32)
            x = resid[rows, :] + extra[rows, :].astype(f32)
            resid[rows, :] = x
            center = x - jnp.sum(x, axis=1, keepdims=True) * (1.0 / width)
            spread = jnp.sum(center * center, axis=1, keepdims=True) * (1.0 / width)
            out[rows, :] = (center * lax.rsqrt(spread + 1e-06) * gains_ref[which : which + 1, :]).astype(bf16)

    norm_to(1, normed, got1)

    def up(c, out):
        up_copy(c).wait()
        out[...] = jnp.dot(normed[...], pool[c], preferred_element_type=f32)

    def gelu(pre, out):
        u = pre[...]
        out[...] = (0.5 * u * (1.0 + lax.erf(u * 0.5**0.5))).astype(bf16)

    def down(c, hid):
        down_copy(c).wait()
        acc[...] += jnp.dot(hid[...], down_buf[c], preferred_element_type=f32)

    acc[...] = jnp.zeros_like(acc)
    up(0, pre_a)
    up(1, pre_b)
    gelu(pre_a, hid_a)
    spare = slots - hidden_chunks
    for m in range(2):
        merge_copy(spare + m).start()

    for c in range(0, hidden_chunks - 2, 2):
        up(c + 2, pre_a)
        gelu(pre_b, hid_b)
        down(c, hid_a)
        merge_copy(spare + c + 2).start()
        up(c + 3, pre_b)
        gelu(pre_a, hid_a)
        down(c + 1, hid_b)
        merge_copy(spare + c + 3).start()

    gelu(pre_b, hid_b)
    down(hidden_chunks - 2, hid_a)
    down_copy(hidden_chunks - 1).wait()
    swaps = []
    for k, (start, size) in enumerate(cuts):
        cols = pl.ds(start, size)
        product = acc[:, cols] + jnp.dot(
            hid_b[...], down_buf[hidden_chunks - 1, :, cols], preferred_element_type=f32
        )
        sent2[:, cols] = product.astype(bf16)
        swap = remote(sent2.at[:, cols], got2.at[:, cols], s2_sems.at[k], r2_sems.at[k])
        swap.start()
        swaps.append(swap)
        resid[:, cols] += product

    row = lax.broadcasted_iota(jnp.int32, (count, count), 0)
    token = lax.broadcasted_iota(jnp.int32, (count, count), 1)
    quarter = count // 4
    part, request, rank = row // quarter, lax.rem(row, quarter) // CAP, lax.rem(row, CAP)
    first = jnp.sum((segment_ref[...] < 1).astype(jnp.int32), axis=1, keepdims=True)
    want = request * first + 4 * rank + part
    pick = jnp.where((token == want) & (segment_ref[...] == request), 1.0, 0.0).astype(bf16)

    def all_but_one(ref):
        return ref.at[pl.ds(0, 63)]

    def wait_all(ref, sem):
        pltpu.make_async_copy(all_but_one(ref), all_but_one(ref), sem).wait()

    wait_all(table, recv_sem_o)
    lanes = lax.broadcasted_iota(jnp.int32, (64, 1, 128), 2)
    sources = lax.broadcasted_iota(jnp.int32, (64, 1, 128), 0)
    inv_v[...] = jnp.max(jnp.where(table[...] == lanes, sources, 0), axis=0)
    to_scalar = pltpu.make_async_copy(inv_v, inv_s, inv_sem)
    to_scalar.start()
    to_scalar.wait()

    for swap in swaps:
        swap.wait()
    norm_to(2, normed, got2)
    for i in range(4):
        merged[:, pl.ds(width * i, width)] = jnp.dot(
            pick[quarter * i : quarter * (i + 1)], normed[...], preferred_element_type=f32
        ).astype(bf16)

    pieces = 4 * out_chunks
    for k, dy in enumerate((2, 3, 1, 0)):
        product = jnp.zeros((quarter, hidden_chunk), f32)
        for i in range(4):
            m = 4 * k + i
            merge_copy(m).wait()
            product += jnp.dot(
                merged[:, pl.ds(width * i, width)], pool[(hidden_chunks + m) % slots], preferred_element_type=f32
            )
            if m + slots < pieces:
                merge_copy(m + slots).start()
        for g in range(4):
            for x in range(4):
                tiles[g * 16 + place.y[dy] * 4 + x] = product[16 * g : 16 * g + 16, 128 * x : 128 * x + 128].astype(bf16)
        for peer in place.others((dy,)):
            pltpu.make_async_remote_copy(
                src_ref=tiles.at[peer], dst_ref=inbox.at[me], send_sem=send_sem_a, recv_sem=recv_sem_a,
                device_id={"req": peer}, device_id_type=MESH,
            ).start()
    inbox[me] = tiles[me]
    wait_all(inbox, recv_sem_a)

    for d in range(64):
        sorted_tiles[d] = inbox[inv_s[0, d]]
    for peer in place.others():
        pltpu.make_async_remote_copy(
            src_ref=sorted_tiles.at[peer], dst_ref=landed.at[me], send_sem=send_sem_b, recv_sem=recv_sem_b,
            device_id={"req": peer}, device_id_type=MESH,
        ).start()
    landed[me] = sorted_tiles[me]
    wait_all(landed, recv_sem_b)
    for g in range(4):
        for c in range(16):
            out_ref[pl.ds(16 * g, 16), pl.ds(128 * c, 128)] = landed[g * 16 + c]
    wait_all(table, send_sem_o)
    wait_all(tiles, send_sem_a)
    wait_all(sorted_tiles, send_sem_b)


def layer(x_t, segment, owner, qkv_t, w_out, w_up, w_down, gains, w_merge):
    width, count = x_t.shape
    half = width // 2
    hidden = w_up.shape[1]
    chunk = 512
    chunks = hidden // chunk
    slots = 12
    heads = half // HEAD_DIM
    rows, out_width = count // 4, w_merge.shape[1]
    f32, bf16 = jnp.float32, jnp.bfloat16
    vmem = pl.BlockSpec(memory_space=pltpu.VMEM)
    smem = pl.BlockSpec(memory_space=pltpu.SMEM)
    anywhere = pl.BlockSpec(memory_space=pl.ANY)
    dma = pltpu.SemaphoreType.DMA
    return pl.pallas_call(
        layer_kernel,
        out_shape=jax.ShapeDtypeStruct((rows, out_width), bf16),
        in_specs=[anywhere, vmem, smem, anywhere, anywhere, anywhere, anywhere, vmem, anywhere],
        out_specs=vmem,
        scratch_shapes=[
            pltpu.VMEM((width, count), bf16),
            pltpu.VMEM((3, half, width), bf16),
            pltpu.VMEM((heads * 128, width), bf16),
            pltpu.VMEM((slots, width, chunk), bf16),
            pltpu.VMEM((chunks, chunk, width), bf16),
            pltpu.VMEM((width, count), bf16),
            pltpu.VMEM((3, heads, 128, count), bf16),
            pltpu.VMEM((count, heads * 128), bf16),
            pltpu.VMEM((count, width), f32),
            pltpu.VMEM((count, width), f32),
            pltpu.VMEM((count, width), bf16),
            pltpu.VMEM((count, chunk), f32),
            pltpu.VMEM((count, chunk), f32),
            pltpu.VMEM((count, chunk), bf16),
            pltpu.VMEM((count, chunk), bf16),
        ]
        + [pltpu.VMEM((count, width), bf16)] * 4
        + [pltpu.VMEM((rows, 4 * width), bf16)]
        + [pltpu.VMEM((64, 16, 128), bf16)] * 4
        + [
            pltpu.VMEM((2, 1, 128), jnp.int32),
            pltpu.VMEM((64, 1, 128), jnp.int32),
            pltpu.VMEM((1, 128), jnp.int32),
            pltpu.SMEM((1, 128), jnp.int32),
        ]
        + [dma, dma((3,)), dma((heads,)), dma((slots,)), dma((chunks,))]
        + [dma((3,))] * 4
        + [dma] * 7,
        compiler_params=pltpu.CompilerParams(
            collective_id=2, has_side_effects=True, vmem_limit_bytes=62 * 1024 * 1024
        ),
        name="layer",
    )(x_t, segment, owner, qkv_t, w_out, w_up, w_down, gains, w_merge)


def local(patches, segment, owner, w_qkv, w_out, w_up, w_down, gains, w_merge):
    x_t = swap_halves(patches.T)
    return layer(
        x_t, segment.reshape(1, -1), owner, w_qkv.transpose(0, 2, 1), w_out, w_up, w_down, gains, w_merge
    )


def solution(mesh):
    in_specs = (
        P("req", "tp"),
        P("req"),
        P("req"),
        P(None, None, "tp"),
        P("tp", None),
        P(None, "tp"),
        P("tp", None),
        P(),
        P(None, "tp"),
    )
    out_specs = P("req", "tp")
    return jax.shard_map(local, mesh=mesh, in_specs=in_specs, out_specs=out_specs, check_vma=False)
```

```python
import functools

import jax
import jax.numpy as jnp
from jax import lax
from jax.experimental import pallas as pl
from jax.experimental.pallas import tpu as pltpu
from jax.sharding import PartitionSpec as P

HEAD_DIM = 104
CAP = 32
MESH = pl.DeviceIdType.MESH


class Place:
    def __init__(self):
        self.me = lax.axis_index("req")
        x, y, z = lax.rem(self.me, 4), lax.rem(self.me // 4, 4), self.me // 16
        self.x = [lax.rem(x + k, 4) for k in range(4)]
        self.y = [lax.rem(y + k, 4) for k in range(4)]
        self.z = [lax.rem(z + k, 4) for k in range(4)]

    def peer(self, dz, dy, dx):
        return self.z[dz] * 16 + self.y[dy] * 4 + self.x[dx]

    def others(self, dys=(2, 3, 1, 0)):
        for dy in dys:
            for dz in (2, 3, 1, 0):
                for dx in (2, 3, 1, 0):
                    if (dz, dy, dx) != (0, 0, 0):
                        yield self.peer(dz, dy, dx)


def swap_kernel(patches_ref, out_ref, x_sem, send_sem, recv_sem):
    tp = lax.axis_index("tp")
    half = patches_ref.shape[0]
    place = out_ref.at[pl.ds(tp * half, half), :]
    mine = pltpu.make_async_copy(patches_ref, place, x_sem)
    mine.start()
    barrier = pltpu.get_barrier_semaphore()
    pl.semaphore_signal(barrier, inc=1, device_id={"tp": 1 - tp}, device_id_type=MESH)
    pl.semaphore_wait(barrier, 1)
    swap = pltpu.make_async_remote_copy(
        src_ref=patches_ref, dst_ref=place, send_sem=send_sem, recv_sem=recv_sem,
        device_id={"tp": 1 - tp}, device_id_type=MESH,
    )
    swap.start()
    mine.wait()
    swap.wait()


def swap_halves(patches_t):
    half, count = patches_t.shape
    dma = pltpu.SemaphoreType.DMA
    return pl.pallas_call(
        swap_kernel,
        out_shape=jax.ShapeDtypeStruct((2 * half, count), patches_t.dtype),
        in_specs=[pl.BlockSpec(memory_space=pltpu.HBM)],
        out_specs=pl.BlockSpec(memory_space=pltpu.VMEM),
        scratch_shapes=[dma, dma, dma],
        compiler_params=pltpu.CompilerParams(
            collective_id=1, has_side_effects=True, vmem_limit_bytes=62 * 1024 * 1024
        ),
        name="swap_halves",
    )(patches_t)


def layer_kernel(
    x_ref, segment_hbm, owner_hbm, qkv_ref, wout_ref, up_ref, down_ref, gains_hbm, merge_ref, out_ref,
    x_t, segment_ref, owner_ref, gains_ref, qkv_buf, wout_buf, pool, down_buf, normed_t, heads, context, resid, acc, normed,
    pre_a, pre_b, hid_a, hid_b, sent, got1, got2,
    merged, tiles, inbox, sorted_tiles, landed, own_rows, table, inv_v, inv_s,
    x_sem, small_sems, qkv_sems, wout_sems, pool_sems, down_sems, s1_sems, r1_sems, s2_sems, r2_sems,
    send_sem_o, recv_sem_o, inv_sem, send_sem_a, recv_sem_a, send_sem_b, recv_sem_b,
):
    f32, bf16 = jnp.float32, jnp.bfloat16
    tp = lax.axis_index("tp")
    partner = {"tp": 1 - tp}
    place = Place()
    me = place.me
    width, count = x_t.shape
    half = width // 2
    head_count = half // HEAD_DIM
    slots, _, hidden_chunk = pool.shape
    hidden_chunks = down_buf.shape[0]
    out_chunks = merge_ref.shape[1] // hidden_chunk
    cuts = [(0, 512), (512, 512), (1024, 640)]

    def qkv_copy(s):
        return pltpu.make_async_copy(qkv_ref.at[s], qkv_buf.at[s], qkv_sems.at[s])

    def wout_copy(h):
        return pltpu.make_async_copy(
            wout_ref.at[pl.ds(HEAD_DIM * h, HEAD_DIM), :], wout_buf.at[pl.ds(128 * h, HEAD_DIM), :], wout_sems.at[h]
        )

    def up_copy(c):
        return pltpu.make_async_copy(
            up_ref.at[:, pl.ds(hidden_chunk * c, hidden_chunk)], pool.at[c], pool_sems.at[c]
        )

    def merge_cols(m):
        return pl.ds(pl.multiple_of(place.y[(2, 3, 1, 0)[m // 4]] * hidden_chunk, hidden_chunk), hidden_chunk)

    def merge_copy(m):
        slot = (hidden_chunks + m) % slots
        return pltpu.make_async_copy(
            merge_ref.at[pl.ds(width * (m % 4), width), merge_cols(m)], pool.at[slot], pool_sems.at[slot]
        )

    def down_copy(c):
        return pltpu.make_async_copy(
            down_ref.at[pl.ds(hidden_chunk * c, hidden_chunk), :], down_buf.at[c], down_sems.at[c]
        )

    def remote(src, dst, send, recv):
        return pltpu.make_async_remote_copy(
            src_ref=src, dst_ref=dst, send_sem=send, recv_sem=recv, device_id=partner, device_id_type=MESH
        )

    x_copy = pltpu.make_async_copy(x_ref, x_t, x_sem)
    small = [
        pltpu.make_async_copy(src, dst, small_sems.at[k])
        for k, (src, dst) in enumerate(
            ((gains_hbm, gains_ref), (segment_hbm, segment_ref), (owner_hbm, owner_ref))
        )
    ]
    x_copy.start()
    for copy in small:
        copy.start()
    for s in range(3):
        qkv_copy(s).start()
    for h in range(head_count):
        wout_copy(h).start()

    barrier = pltpu.get_barrier_semaphore()
    for peer in place.others():
        pl.semaphore_signal(barrier, inc=1, device_id={"req": peer}, device_id_type=MESH)
    pl.semaphore_signal(barrier, inc=1, device_id=partner, device_id_type=MESH)

    for copy in small:
        copy.wait()
    for j in range(2):
        own_rows[j] = jnp.full((1, 128), owner_ref[j], jnp.int32)
    for h in range(head_count):
        wout_buf[pl.ds(128 * h + HEAD_DIM, 128 - HEAD_DIM), :] = jnp.zeros((128 - HEAD_DIM, width), bf16)
        for s in range(3):
            heads[s, h, pl.ds(HEAD_DIM, 128 - HEAD_DIM), :] = jnp.zeros((128 - HEAD_DIM, count), bf16)
    seg_rows = jnp.broadcast_to(segment_ref[...], (count, count))
    same = seg_rows == seg_rows.T

    x_copy.wait()
    total = jnp.zeros((1, count), f32)
    for b in range(width // 128):
        total += jnp.sum(x_t[pl.ds(128 * b, 128), :].astype(f32), axis=0, keepdims=True)
    mean = total * (1.0 / width)
    total = jnp.zeros((1, count), f32)
    for b in range(width // 128):
        center = x_t[pl.ds(128 * b, 128), :].astype(f32) - mean
        total += jnp.sum(center * center, axis=0, keepdims=True)
    scale = lax.rsqrt(total * (1.0 / width) + 1e-06)
    for b in range(width // 128):
        gain = jnp.broadcast_to(gains_ref[0:1, pl.ds(128 * b, 128)], (128, 128)).T
        gain = jnp.concatenate([gain] * (count // 128), axis=1)
        x = x_t[pl.ds(128 * b, 128), :].astype(f32)
        normed_t[pl.ds(128 * b, 128), :] = ((x - mean) * scale * gain).astype(bf16)

    for s in range(3):
        qkv_copy(s).wait()
        for c in range(s * 3, min(s * 3 + 3, hidden_chunks)):
            up_copy(c).start()
            down_copy(c).start()
        if s == 2:
            for m in range(slots - hidden_chunks):
                merge_copy(m).start()
        product = jnp.dot(qkv_buf[s], normed_t[...], preferred_element_type=f32)
        for h in range(head_count):
            heads[s, h, pl.ds(0, HEAD_DIM), :] = product[HEAD_DIM * h : HEAD_DIM * (h + 1)].astype(bf16)

    for h in range(head_count):
        scores = lax.dot_general(
            heads[1, h], heads[0, h], (((0,), (0,)), ((), ())), preferred_element_type=f32
        )
        scores = jnp.where(same, scores * HEAD_DIM ** (-0.5), -1e30)
        top = jnp.max(scores, axis=0, keepdims=True)
        expo = jnp.exp(scores - top)
        share = 1.0 / jnp.sum(expo, axis=0, keepdims=True)
        mixed = jnp.dot(heads[2, h], expo.astype(bf16), preferred_element_type=f32) * share
        context[:, pl.ds(128 * h, 128)] = mixed.T.astype(bf16)

    for h in range(head_count):
        wout_copy(h).wait()
    pl.semaphore_wait(barrier, 64)
    swaps = []
    for k, (start, size) in enumerate(cuts):
        cols = pl.ds(start, size)
        product = jnp.dot(context[...], wout_buf[:, cols], preferred_element_type=f32)
        sent[:, cols] = product.astype(bf16)
        swap = remote(sent.at[:, cols], got1.at[:, cols], s1_sems.at[k], r1_sems.at[k])
        swap.start()
        swaps.append(swap)
        resid[:, cols] = product + x_t[cols, :].astype(f32).T

    for peer in place.others():
        pltpu.make_async_remote_copy(
            src_ref=own_rows.at[peer // 32], dst_ref=table.at[me], send_sem=send_sem_o, recv_sem=recv_sem_o,
            device_id={"req": peer}, device_id_type=MESH,
        ).start()
    table[me] = own_rows[me // 32]

    for swap in swaps:
        swap.wait()

    def norm_to(which, out, extra):
        for b in range(count // 32):
            rows = pl.ds(32 * b, 32)
            x = resid[rows, :] + extra[rows, :].astype(f32)
            resid[rows, :] = x
            center = x - jnp.sum(x, axis=1, keepdims=True) * (1.0 / width)
            spread = jnp.sum(center * center, axis=1, keepdims=True) * (1.0 / width)
            out[rows, :] = (center * lax.rsqrt(spread + 1e-06) * gains_ref[which : which + 1, :]).astype(bf16)

    norm_to(1, normed, got1)

    def up(c, out):
        out[...] = jnp.dot(normed[...], pool[c], preferred_element_type=f32)

    def gelu(pre, out):
        u = pre[...]
        out[...] = (0.5 * u * (1.0 + lax.erf(u * 0.5**0.5))).astype(bf16)

    def down(c, hid):
        acc[...] += jnp.dot(hid[...], down_buf[c], preferred_element_type=f32)

    def wait_chunks(chunks):
        for c in chunks:
            up_copy(c).wait()
            down_copy(c).wait()

    acc[...] = jnp.zeros_like(acc)
    spare = slots - hidden_chunks
    middle = hidden_chunks // 2
    wait_chunks(range(middle))
    up(0, pre_a)
    up(1, pre_b)
    gelu(pre_a, hid_a)
    for c in range(0, hidden_chunks - 2, 2):
        if c + 2 == middle:
            wait_chunks(range(middle, hidden_chunks))
            for m in range(middle):
                merge_copy(spare + m).start()
        up(c + 2, pre_a)
        gelu(pre_b, hid_b)
        down(c, hid_a)
        up(c + 3, pre_b)
        gelu(pre_a, hid_a)
        down(c + 1, hid_b)

    for m in range(middle, hidden_chunks):
        merge_copy(spare + m).start()
    gelu(pre_b, hid_b)
    down(hidden_chunks - 2, hid_a)
    swaps = []
    for k, (start, size) in enumerate(cuts):
        cols = pl.ds(start, size)
        product = acc[:, cols] + jnp.dot(
            hid_b[...], down_buf[hidden_chunks - 1, :, cols], preferred_element_type=f32
        )
        sent[:, cols] = product.astype(bf16)
        swap = remote(sent.at[:, cols], got2.at[:, cols], s2_sems.at[k], r2_sems.at[k])
        swap.start()
        swaps.append(swap)
        resid[:, cols] += product

    row = lax.broadcasted_iota(jnp.int32, (count, count), 0)
    token = lax.broadcasted_iota(jnp.int32, (count, count), 1)
    quarter = count // 4
    part, request, rank = row // quarter, lax.rem(row, quarter) // CAP, lax.rem(row, CAP)
    first = jnp.sum((segment_ref[...] < 1).astype(jnp.int32), axis=1, keepdims=True)
    want = request * first + 4 * rank + part
    pick = jnp.where((token == want) & (segment_ref[...] == request), 1.0, 0.0).astype(bf16)

    def all_but_one(ref):
        return ref.at[pl.ds(0, 63)]

    def wait_all(ref, sem):
        pltpu.make_async_copy(all_but_one(ref), all_but_one(ref), sem).wait()

    wait_all(table, recv_sem_o)
    lanes = lax.broadcasted_iota(jnp.int32, (64, 1, 128), 2)
    sources = lax.broadcasted_iota(jnp.int32, (64, 1, 128), 0)
    inv_v[...] = jnp.max(jnp.where(table[...] == lanes, sources, 0), axis=0)
    to_scalar = pltpu.make_async_copy(inv_v, inv_s, inv_sem)
    to_scalar.start()
    to_scalar.wait()

    for swap in swaps:
        swap.wait()
    norm_to(2, normed, got2)
    for i in range(4):
        merged[:, pl.ds(width * i, width)] = jnp.dot(
            pick[quarter * i : quarter * (i + 1)], normed[...], preferred_element_type=f32
        ).astype(bf16)

    pieces = 4 * out_chunks
    for m in range(spare + hidden_chunks):
        merge_copy(m).wait()
    for k, dy in enumerate((2, 3, 1, 0)):
        for m in range(spare + hidden_chunks, 4 * k + 4):
            merge_copy(m).wait()
        product = jnp.zeros((quarter, hidden_chunk), f32)
        for i in range(4):
            m = 4 * k + i
            product += jnp.dot(
                merged[:, pl.ds(width * i, width)], pool[(hidden_chunks + m) % slots], preferred_element_type=f32
            )
        for i in range(4):
            m = 4 * k + i + slots
            if m < pieces:
                merge_copy(m).start()
        for g in range(4):
            for x in range(4):
                tiles[g * 16 + place.y[dy] * 4 + x] = product[16 * g : 16 * g + 16, 128 * x : 128 * x + 128].astype(bf16)
        for peer in place.others((dy,)):
            pltpu.make_async_remote_copy(
                src_ref=tiles.at[peer], dst_ref=inbox.at[me], send_sem=send_sem_a, recv_sem=recv_sem_a,
                device_id={"req": peer}, device_id_type=MESH,
            ).start()
    inbox[me] = tiles[me]
    wait_all(inbox, recv_sem_a)

    for d in range(64):
        sorted_tiles[d] = inbox[inv_s[0, d]]
    for peer in place.others():
        pltpu.make_async_remote_copy(
            src_ref=sorted_tiles.at[peer], dst_ref=landed.at[me], send_sem=send_sem_b, recv_sem=recv_sem_b,
            device_id={"req": peer}, device_id_type=MESH,
        ).start()
    landed[me] = sorted_tiles[me]
    wait_all(landed, recv_sem_b)
    for g in range(4):
        for c in range(16):
            out_ref[pl.ds(16 * g, 16), pl.ds(128 * c, 128)] = landed[g * 16 + c]
    wait_all(table, send_sem_o)
    wait_all(tiles, send_sem_a)
    wait_all(sorted_tiles, send_sem_b)


def layer(x_t, segment, owner, qkv_t, w_out, w_up, w_down, gains, w_merge):
    width, count = x_t.shape
    half = width // 2
    hidden = w_up.shape[1]
    chunk = 512
    chunks = hidden // chunk
    slots = 14
    heads = half // HEAD_DIM
    rows, out_width = count // 4, w_merge.shape[1]
    f32, bf16 = jnp.float32, jnp.bfloat16
    vmem = pl.BlockSpec(memory_space=pltpu.VMEM)
    hbm = pl.BlockSpec(memory_space=pltpu.HBM)
    dma = pltpu.SemaphoreType.DMA
    return pl.pallas_call(
        layer_kernel,
        out_shape=jax.ShapeDtypeStruct((rows, out_width), bf16),
        in_specs=[hbm] * 9,
        out_specs=vmem,
        scratch_shapes=[
            pltpu.VMEM((width, count), bf16),
            pltpu.VMEM((1, count), jnp.int32),
            pltpu.SMEM((2,), jnp.int32),
            pltpu.VMEM((3, width), f32),
            pltpu.VMEM((3, half, width), bf16),
            pltpu.VMEM((heads * 128, width), bf16),
            pltpu.VMEM((slots, width, chunk), bf16),
            pltpu.VMEM((chunks, chunk, width), bf16),
            pltpu.VMEM((width, count), bf16),
            pltpu.VMEM((3, heads, 128, count), bf16),
            pltpu.VMEM((count, heads * 128), bf16),
            pltpu.VMEM((count, width), f32),
            pltpu.VMEM((count, width), f32),
            pltpu.VMEM((count, width), bf16),
            pltpu.VMEM((count, chunk), f32),
            pltpu.VMEM((count, chunk), f32),
            pltpu.VMEM((count, chunk), bf16),
            pltpu.VMEM((count, chunk), bf16),
        ]
        + [pltpu.VMEM((count, width), bf16)] * 3
        + [pltpu.VMEM((rows, 4 * width), bf16)]
        + [pltpu.VMEM((64, 16, 128), bf16)] * 4
        + [
            pltpu.VMEM((2, 1, 128), jnp.int32),
            pltpu.VMEM((64, 1, 128), jnp.int32),
            pltpu.VMEM((1, 128), jnp.int32),
            pltpu.SMEM((1, 128), jnp.int32),
        ]
        + [dma, dma((3,)), dma((3,)), dma((heads,)), dma((slots,)), dma((chunks,))]
        + [dma((3,))] * 4
        + [dma] * 7,
        compiler_params=pltpu.CompilerParams(
            collective_id=2, has_side_effects=True, vmem_limit_bytes=62 * 1024 * 1024
        ),
        name="layer",
    )(x_t, segment, owner, qkv_t, w_out, w_up, w_down, gains, w_merge)


def local(patches, segment, owner, w_qkv, w_out, w_up, w_down, gains, w_merge):
    x_t = swap_halves(patches.T)
    return layer(
        x_t, segment.reshape(1, -1), owner, w_qkv.transpose(0, 2, 1), w_out, w_up, w_down, gains, w_merge
    )


def solution(mesh):
    in_specs = (
        P("req", "tp"),
        P("req"),
        P("req"),
        P(None, None, "tp"),
        P("tp", None),
        P(None, "tp"),
        P("tp", None),
        P(),
        P(None, "tp"),
    )
    out_specs = P("req", "tp")
    return jax.shard_map(local, mesh=mesh, in_specs=in_specs, out_specs=out_specs, check_vma=False)
```

```python
import functools

import jax
import jax.numpy as jnp
from jax import lax
from jax.experimental import pallas as pl
from jax.experimental.pallas import tpu as pltpu
from jax.sharding import PartitionSpec as P

HEAD_DIM = 104
CAP = 32
MESH = pl.DeviceIdType.MESH


class Place:
    def __init__(self):
        self.me = lax.axis_index("req")
        x, y, z = lax.rem(self.me, 4), lax.rem(self.me // 4, 4), self.me // 16
        self.x = [lax.rem(x + k, 4) for k in range(4)]
        self.y = [lax.rem(y + k, 4) for k in range(4)]
        self.z = [lax.rem(z + k, 4) for k in range(4)]

    def peer(self, dz, dy, dx):
        return self.z[dz] * 16 + self.y[dy] * 4 + self.x[dx]

    def others(self, dys=(2, 3, 1, 0)):
        for dy in dys:
            for dz in (2, 3, 1, 0):
                for dx in (2, 3, 1, 0):
                    if (dz, dy, dx) != (0, 0, 0):
                        yield self.peer(dz, dy, dx)


def swap_kernel(patches_ref, out_ref, x_sem, send_sem, recv_sem):
    tp = lax.axis_index("tp")
    half = patches_ref.shape[0]
    place = out_ref.at[pl.ds(tp * half, half), :]
    mine = pltpu.make_async_copy(patches_ref, place, x_sem)
    mine.start()
    barrier = pltpu.get_barrier_semaphore()
    pl.semaphore_signal(barrier, inc=1, device_id={"tp": 1 - tp}, device_id_type=MESH)
    pl.semaphore_wait(barrier, 1)
    swap = pltpu.make_async_remote_copy(
        src_ref=patches_ref, dst_ref=place, send_sem=send_sem, recv_sem=recv_sem,
        device_id={"tp": 1 - tp}, device_id_type=MESH,
    )
    swap.start()
    mine.wait()
    swap.wait()


def swap_halves(patches_t):
    half, count = patches_t.shape
    dma = pltpu.SemaphoreType.DMA
    return pl.pallas_call(
        swap_kernel,
        out_shape=jax.ShapeDtypeStruct((2 * half, count), patches_t.dtype),
        in_specs=[pl.BlockSpec(memory_space=pltpu.HBM)],
        out_specs=pl.BlockSpec(memory_space=pltpu.VMEM),
        scratch_shapes=[dma, dma, dma],
        compiler_params=pltpu.CompilerParams(
            collective_id=1, has_side_effects=True, vmem_limit_bytes=62 * 1024 * 1024
        ),
        name="swap_halves",
    )(patches_t)


def layer_kernel(
    x_ref, segment_hbm, owner_hbm, qkv_ref, wout_ref, up_ref, down_ref, gains_hbm, merge_ref, out_ref,
    x_t, segment_ref, owner_ref, gains_ref, qkv_buf, wout_buf, pool, down_buf, normed_t, heads, context, resid, acc, normed,
    pre_a, pre_b, hid_a, hid_b, sent, got1, got2,
    merged, tiles, inbox, sorted_tiles, landed, own_rows, table, inv_v, inv_s,
    x_sem, small_sems, qkv_sems, wout_sems, pool_sems, down_sems, s1_sems, r1_sems, s2_sems, r2_sems,
    send_sem_o, recv_sem_o, inv_sem, send_sem_a, recv_sem_a, send_sem_b, recv_sem_b,
):
    f32, bf16 = jnp.float32, jnp.bfloat16
    tp = lax.axis_index("tp")
    partner = {"tp": 1 - tp}
    place = Place()
    me = place.me
    width, count = x_t.shape
    half = width // 2
    head_count = half // HEAD_DIM
    slots, _, hidden_chunk = pool.shape
    hidden_chunks = down_ref.shape[0] // hidden_chunk
    middle = hidden_chunks // 2
    spare = slots - hidden_chunks
    cuts = [(0, 512), (512, 512), (1024, 640)]

    def qkv_copy(s):
        return pltpu.make_async_copy(qkv_ref.at[s], qkv_buf.at[s], qkv_sems.at[s])

    def wout_copy(h):
        return pltpu.make_async_copy(
            wout_ref.at[pl.ds(HEAD_DIM * h, HEAD_DIM), :], wout_buf.at[pl.ds(128 * h, HEAD_DIM), :], wout_sems.at[h]
        )

    def up_copy(c):
        return pltpu.make_async_copy(
            up_ref.at[:, pl.ds(hidden_chunk * c, hidden_chunk)], pool.at[c], pool_sems.at[c]
        )

    def merge_cols(m):
        return pl.ds(pl.multiple_of(place.y[(2, 3, 1, 0)[m // 4]] * hidden_chunk, hidden_chunk), hidden_chunk)

    def merge_copy(m):
        slot = (hidden_chunks + m) % slots
        return pltpu.make_async_copy(
            merge_ref.at[pl.ds(width * (m % 4), width), merge_cols(m)], pool.at[slot], pool_sems.at[slot]
        )

    def down_place(c):
        if c < 3:
            return down_buf.at[c]
        if c in (4, 5):
            return wout_buf.at[pl.ds(hidden_chunk * (c - 4), hidden_chunk), :]
        return qkv_buf.at[{3: 2, 6: 0, 7: 1}[c], pl.ds(0, hidden_chunk), :]

    def down_copy(c):
        return pltpu.make_async_copy(
            down_ref.at[pl.ds(hidden_chunk * c, hidden_chunk), :], down_place(c), down_sems.at[c]
        )

    def remote(src, dst, send, recv):
        return pltpu.make_async_remote_copy(
            src_ref=src, dst_ref=dst, send_sem=send, recv_sem=recv, device_id=partner, device_id_type=MESH
        )

    x_copy = pltpu.make_async_copy(x_ref, x_t, x_sem)
    small = [
        pltpu.make_async_copy(src, dst, small_sems.at[k])
        for k, (src, dst) in enumerate(
            ((gains_hbm, gains_ref), (segment_hbm, segment_ref), (owner_hbm, owner_ref))
        )
    ]
    x_copy.start()
    for copy in small:
        copy.start()
    for s in range(3):
        qkv_copy(s).start()
    for h in range(head_count):
        wout_copy(h).start()

    barrier = pltpu.get_barrier_semaphore()
    for peer in place.others():
        pl.semaphore_signal(barrier, inc=1, device_id={"req": peer}, device_id_type=MESH)
    pl.semaphore_signal(barrier, inc=1, device_id=partner, device_id_type=MESH)

    for copy in small:
        copy.wait()
    for j in range(2):
        own_rows[j] = jnp.full((1, 128), owner_ref[j], jnp.int32)
    for h in range(head_count):
        wout_buf[pl.ds(128 * h + HEAD_DIM, 128 - HEAD_DIM), :] = jnp.zeros((128 - HEAD_DIM, width), bf16)
        for s in range(3):
            heads[s, h, pl.ds(HEAD_DIM, 128 - HEAD_DIM), :] = jnp.zeros((128 - HEAD_DIM, count), bf16)
    seg_rows = jnp.broadcast_to(segment_ref[...], (count, count))
    same = seg_rows == seg_rows.T

    x_copy.wait()
    total = jnp.zeros((1, count), f32)
    for b in range(width // 128):
        total += jnp.sum(x_t[pl.ds(128 * b, 128), :].astype(f32), axis=0, keepdims=True)
    mean = total * (1.0 / width)
    total = jnp.zeros((1, count), f32)
    for b in range(width // 128):
        center = x_t[pl.ds(128 * b, 128), :].astype(f32) - mean
        total += jnp.sum(center * center, axis=0, keepdims=True)
    scale = lax.rsqrt(total * (1.0 / width) + 1e-06)
    for b in range(width // 128):
        gain = jnp.broadcast_to(gains_ref[0:1, pl.ds(128 * b, 128)], (128, 128)).T
        gain = jnp.concatenate([gain] * (count // 128), axis=1)
        x = x_t[pl.ds(128 * b, 128), :].astype(f32)
        normed_t[pl.ds(128 * b, 128), :] = ((x - mean) * scale * gain).astype(bf16)

    for s in range(3):
        qkv_copy(s).wait()
        for c in range(2 * s, min(2 * s + 2, middle)):
            up_copy(c).start()
            if c < 3:
                down_copy(c).start()
        product = jnp.dot(qkv_buf[s], normed_t[...], preferred_element_type=f32)
        for h in range(head_count):
            heads[s, h, pl.ds(0, HEAD_DIM), :] = product[HEAD_DIM * h : HEAD_DIM * (h + 1)].astype(bf16)
    down_copy(3).start()

    for h in range(head_count):
        scores = lax.dot_general(
            heads[1, h], heads[0, h], (((0,), (0,)), ((), ())), preferred_element_type=f32
        )
        scores = jnp.where(same, scores * HEAD_DIM ** (-0.5), -1e30)
        top = jnp.max(scores, axis=0, keepdims=True)
        expo = jnp.exp(scores - top)
        share = 1.0 / jnp.sum(expo, axis=0, keepdims=True)
        mixed = jnp.dot(heads[2, h], expo.astype(bf16), preferred_element_type=f32) * share
        context[:, pl.ds(128 * h, 128)] = mixed.T.astype(bf16)

    for h in range(head_count):
        wout_copy(h).wait()
    pl.semaphore_wait(barrier, 64)
    swaps = []
    for k, (start, size) in enumerate(cuts):
        cols = pl.ds(start, size)
        product = jnp.dot(context[...], wout_buf[:, cols], preferred_element_type=f32)
        sent[:, cols] = product.astype(bf16)
        swap = remote(sent.at[:, cols], got1.at[:, cols], s1_sems.at[k], r1_sems.at[k])
        swap.start()
        swaps.append(swap)
        resid[:, cols] = product + x_t[cols, :].astype(f32).T

    for c in range(middle, hidden_chunks):
        up_copy(c).start()
        down_copy(c).start()

    for peer in place.others():
        pltpu.make_async_remote_copy(
            src_ref=own_rows.at[peer // 32], dst_ref=table.at[me], send_sem=send_sem_o, recv_sem=recv_sem_o,
            device_id={"req": peer}, device_id_type=MESH,
        ).start()
    table[me] = own_rows[me // 32]

    for swap in swaps:
        swap.wait()

    def norm_to(which, out, extra):
        for b in range(count // 32):
            rows = pl.ds(32 * b, 32)
            x = resid[rows, :] + extra[rows, :].astype(f32)
            resid[rows, :] = x
            center = x - jnp.sum(x, axis=1, keepdims=True) * (1.0 / width)
            spread = jnp.sum(center * center, axis=1, keepdims=True) * (1.0 / width)
            out[rows, :] = (center * lax.rsqrt(spread + 1e-06) * gains_ref[which : which + 1, :]).astype(bf16)

    norm_to(1, normed, got1)

    def up(c, out):
        out[...] = jnp.dot(normed[...], pool[c], preferred_element_type=f32)

    def gelu(pre, out):
        u = pre[...]
        out[...] = (0.5 * u * (1.0 + lax.erf(u * 0.5**0.5))).astype(bf16)

    def down(c, hid):
        acc[...] += jnp.dot(hid[...], down_place(c)[...], preferred_element_type=f32)

    def wait_chunks(chunks):
        for c in chunks:
            up_copy(c).wait()
            down_copy(c).wait()

    acc[...] = jnp.zeros_like(acc)
    wait_chunks(range(middle))
    for m in range(spare):
        merge_copy(m).start()
    up(0, pre_a)
    up(1, pre_b)
    gelu(pre_a, hid_a)
    for c in range(0, hidden_chunks - 2, 2):
        if c + 2 == middle:
            wait_chunks(range(middle, hidden_chunks))
            for m in range(middle):
                merge_copy(spare + m).start()
        up(c + 2, pre_a)
        gelu(pre_b, hid_b)
        down(c, hid_a)
        up(c + 3, pre_b)
        gelu(pre_a, hid_a)
        down(c + 1, hid_b)

    gelu(pre_b, hid_b)
    down(hidden_chunks - 2, hid_a)
    swaps = []
    for k, (start, size) in enumerate(cuts):
        cols = pl.ds(start, size)
        product = acc[:, cols] + jnp.dot(
            hid_b[...], down_place(hidden_chunks - 1)[:, cols], preferred_element_type=f32
        )
        sent[:, cols] = product.astype(bf16)
        swap = remote(sent.at[:, cols], got2.at[:, cols], s2_sems.at[k], r2_sems.at[k])
        swap.start()
        swaps.append(swap)
        resid[:, cols] += product
    for m in range(middle, hidden_chunks):
        merge_copy(spare + m).start()

    row = lax.broadcasted_iota(jnp.int32, (count, count), 0)
    token = lax.broadcasted_iota(jnp.int32, (count, count), 1)
    quarter = count // 4
    part, request, rank = row // quarter, lax.rem(row, quarter) // CAP, lax.rem(row, CAP)
    first = jnp.sum((segment_ref[...] < 1).astype(jnp.int32), axis=1, keepdims=True)
    want = request * first + 4 * rank + part
    pick = jnp.where((token == want) & (segment_ref[...] == request), 1.0, 0.0).astype(bf16)

    def all_but_one(ref):
        return ref.at[pl.ds(0, 63)]

    def wait_all(ref, sem):
        pltpu.make_async_copy(all_but_one(ref), all_but_one(ref), sem).wait()

    wait_all(table, recv_sem_o)
    lanes = lax.broadcasted_iota(jnp.int32, (64, 1, 128), 2)
    sources = lax.broadcasted_iota(jnp.int32, (64, 1, 128), 0)
    inv_v[...] = jnp.max(jnp.where(table[...] == lanes, sources, 0), axis=0)
    to_scalar = pltpu.make_async_copy(inv_v, inv_s, inv_sem)
    to_scalar.start()
    to_scalar.wait()

    for swap in swaps:
        swap.wait()
    norm_to(2, normed, got2)
    for i in range(4):
        merged[:, pl.ds(width * i, width)] = jnp.dot(
            pick[quarter * i : quarter * (i + 1)], normed[...], preferred_element_type=f32
        ).astype(bf16)

    for k, dy in enumerate((2, 3, 1, 0)):
        for i in range(4):
            merge_copy(4 * k + i).wait()
        product = jnp.zeros((quarter, hidden_chunk), f32)
        for i in range(4):
            m = 4 * k + i
            product += jnp.dot(
                merged[:, pl.ds(width * i, width)], pool[(hidden_chunks + m) % slots], preferred_element_type=f32
            )
        for g in range(4):
            for x in range(4):
                tiles[g * 16 + place.y[dy] * 4 + x] = product[16 * g : 16 * g + 16, 128 * x : 128 * x + 128].astype(bf16)
        for peer in place.others((dy,)):
            pltpu.make_async_remote_copy(
                src_ref=tiles.at[peer], dst_ref=inbox.at[me], send_sem=send_sem_a, recv_sem=recv_sem_a,
                device_id={"req": peer}, device_id_type=MESH,
            ).start()
    inbox[me] = tiles[me]
    wait_all(inbox, recv_sem_a)

    for d in range(64):
        sorted_tiles[d] = inbox[inv_s[0, d]]
    for peer in place.others():
        pltpu.make_async_remote_copy(
            src_ref=sorted_tiles.at[peer], dst_ref=landed.at[me], send_sem=send_sem_b, recv_sem=recv_sem_b,
            device_id={"req": peer}, device_id_type=MESH,
        ).start()
    landed[me] = sorted_tiles[me]
    wait_all(landed, recv_sem_b)
    for g in range(4):
        for c in range(16):
            out_ref[pl.ds(16 * g, 16), pl.ds(128 * c, 128)] = landed[g * 16 + c]
    wait_all(table, send_sem_o)
    wait_all(tiles, send_sem_a)
    wait_all(sorted_tiles, send_sem_b)


def layer(x_t, segment, owner, qkv_t, w_out, w_up, w_down, gains, w_merge):
    width, count = x_t.shape
    half = width // 2
    hidden = w_up.shape[1]
    chunk = 512
    chunks = hidden // chunk
    slots = 16
    heads = half // HEAD_DIM
    rows, out_width = count // 4, w_merge.shape[1]
    f32, bf16 = jnp.float32, jnp.bfloat16
    vmem = pl.BlockSpec(memory_space=pltpu.VMEM)
    hbm = pl.BlockSpec(memory_space=pltpu.HBM)
    dma = pltpu.SemaphoreType.DMA
    return pl.pallas_call(
        layer_kernel,
        out_shape=jax.ShapeDtypeStruct((rows, out_width), bf16),
        in_specs=[hbm] * 9,
        out_specs=vmem,
        scratch_shapes=[
            pltpu.VMEM((width, count), bf16),
            pltpu.VMEM((1, count), jnp.int32),
            pltpu.SMEM((2,), jnp.int32),
            pltpu.VMEM((3, width), f32),
            pltpu.VMEM((3, half, width), bf16),
            pltpu.VMEM((heads * 128, width), bf16),
            pltpu.VMEM((slots, width, chunk), bf16),
            pltpu.VMEM((3, chunk, width), bf16),
            pltpu.VMEM((width, count), bf16),
            pltpu.VMEM((3, heads, 128, count), bf16),
            pltpu.VMEM((count, heads * 128), bf16),
            pltpu.VMEM((count, width), f32),
            pltpu.VMEM((count, width), f32),
            pltpu.VMEM((count, width), bf16),
            pltpu.VMEM((count, chunk), f32),
            pltpu.VMEM((count, chunk), f32),
            pltpu.VMEM((count, chunk), bf16),
            pltpu.VMEM((count, chunk), bf16),
        ]
        + [pltpu.VMEM((count, width), bf16)] * 3
        + [pltpu.VMEM((rows, 4 * width), bf16)]
        + [pltpu.VMEM((64, 16, 128), bf16)] * 4
        + [
            pltpu.VMEM((2, 1, 128), jnp.int32),
            pltpu.VMEM((64, 1, 128), jnp.int32),
            pltpu.VMEM((1, 128), jnp.int32),
            pltpu.SMEM((1, 128), jnp.int32),
        ]
        + [dma, dma((3,)), dma((3,)), dma((heads,)), dma((slots,)), dma((chunks,))]
        + [dma((3,))] * 4
        + [dma] * 7,
        compiler_params=pltpu.CompilerParams(
            collective_id=2, has_side_effects=True, vmem_limit_bytes=62 * 1024 * 1024
        ),
        name="layer",
    )(x_t, segment, owner, qkv_t, w_out, w_up, w_down, gains, w_merge)


def local(patches, segment, owner, w_qkv, w_out, w_up, w_down, gains, w_merge):
    x_t = swap_halves(patches.T)
    return layer(
        x_t, segment.reshape(1, -1), owner, w_qkv.transpose(0, 2, 1), w_out, w_up, w_down, gains, w_merge
    )


def solution(mesh):
    in_specs = (
        P("req", "tp"),
        P("req"),
        P("req"),
        P(None, None, "tp"),
        P("tp", None),
        P(None, "tp"),
        P("tp", None),
        P(),
        P(None, "tp"),
    )
    out_specs = P("req", "tp")
    return jax.shard_map(local, mesh=mesh, in_specs=in_specs, out_specs=out_specs, check_vma=False)
```

```python
import functools

import jax
import jax.numpy as jnp
from jax import lax
from jax.experimental import pallas as pl
from jax.experimental.pallas import tpu as pltpu
from jax.sharding import PartitionSpec as P

HEAD_DIM = 104
CAP = 32
MESH = pl.DeviceIdType.MESH


class Place:
    def __init__(self):
        self.me = lax.axis_index("req")
        x, y, z = lax.rem(self.me, 4), lax.rem(self.me // 4, 4), self.me // 16
        self.x = [lax.rem(x + k, 4) for k in range(4)]
        self.y = [lax.rem(y + k, 4) for k in range(4)]
        self.z = [lax.rem(z + k, 4) for k in range(4)]

    def peer(self, dz, dy, dx):
        return self.z[dz] * 16 + self.y[dy] * 4 + self.x[dx]

    def others(self, dys=(2, 3, 1, 0)):
        for dy in dys:
            for dz in (2, 3, 1, 0):
                for dx in (2, 3, 1, 0):
                    if (dz, dy, dx) != (0, 0, 0):
                        yield self.peer(dz, dy, dx)


def swap_kernel(patches_ref, out_ref, x_sem, send_sem, recv_sem):
    tp = lax.axis_index("tp")
    half = patches_ref.shape[0]
    place = out_ref.at[pl.ds(tp * half, half), :]
    mine = pltpu.make_async_copy(patches_ref, place, x_sem)
    mine.start()
    barrier = pltpu.get_barrier_semaphore()
    pl.semaphore_signal(barrier, inc=1, device_id={"tp": 1 - tp}, device_id_type=MESH)
    pl.semaphore_wait(barrier, 1)
    swap = pltpu.make_async_remote_copy(
        src_ref=patches_ref, dst_ref=place, send_sem=send_sem, recv_sem=recv_sem,
        device_id={"tp": 1 - tp}, device_id_type=MESH,
    )
    swap.start()
    mine.wait()
    swap.wait()


def swap_halves(patches_t):
    half, count = patches_t.shape
    dma = pltpu.SemaphoreType.DMA
    return pl.pallas_call(
        swap_kernel,
        out_shape=jax.ShapeDtypeStruct((2 * half, count), patches_t.dtype),
        in_specs=[pl.BlockSpec(memory_space=pltpu.HBM)],
        out_specs=pl.BlockSpec(memory_space=pltpu.VMEM),
        scratch_shapes=[dma, dma, dma],
        compiler_params=pltpu.CompilerParams(
            collective_id=1, has_side_effects=True, vmem_limit_bytes=62 * 1024 * 1024
        ),
        name="swap_halves",
    )(patches_t)


def layer_kernel(
    x_ref, segment_hbm, owner_hbm, qkv_ref, wout_ref, up_ref, down_ref, gains_hbm, merge_ref, out_ref,
    x_t, segment_ref, owner_ref, gains_ref, qkv_buf, wout_buf, pool, down_buf, normed_t, heads, context, resid, acc, normed,
    pre_a, pre_b, hid_a, hid_b, sent, got1, got2,
    merged, tiles, inbox, sorted_tiles, landed, own_rows, table, inv_v, inv_s,
    x_sem, small_sems, qkv_sems, wout_sems, pool_sems, down_sems, s1_sems, r1_sems, s2_sems, r2_sems,
    send_sem_o, recv_sem_o, inv_sem, send_sem_a, recv_sem_a, send_sem_b, recv_sem_b,
):
    f32, bf16 = jnp.float32, jnp.bfloat16
    tp = lax.axis_index("tp")
    partner = {"tp": 1 - tp}
    place = Place()
    me = place.me
    width, count = x_t.shape
    half = width // 2
    head_count = half // HEAD_DIM
    slots, _, hidden_chunk = pool.shape
    hidden_chunks = down_ref.shape[0] // hidden_chunk
    middle = hidden_chunks // 2
    spare = slots - hidden_chunks
    cuts = [(0, 512), (512, 512), (1024, 640)]

    def qkv_copy(s):
        return pltpu.make_async_copy(qkv_ref.at[s], qkv_buf.at[s], qkv_sems.at[s])

    def wout_copy(h):
        return pltpu.make_async_copy(
            wout_ref.at[pl.ds(HEAD_DIM * h, HEAD_DIM), :], wout_buf.at[pl.ds(128 * h, HEAD_DIM), :], wout_sems.at[h]
        )

    def up_copy(c):
        return pltpu.make_async_copy(
            up_ref.at[:, pl.ds(hidden_chunk * c, hidden_chunk)], pool.at[c], pool_sems.at[c]
        )

    def merge_cols(m):
        return pl.ds(pl.multiple_of(place.y[(2, 3, 1, 0)[m // 4]] * hidden_chunk, hidden_chunk), hidden_chunk)

    def merge_copy(m):
        slot = (hidden_chunks + m) % slots
        return pltpu.make_async_copy(
            merge_ref.at[pl.ds(width * (m % 4), width), merge_cols(m)], pool.at[slot], pool_sems.at[slot]
        )

    def down_place(c):
        if c < 3:
            return down_buf.at[c]
        if c in (4, 5):
            return wout_buf.at[pl.ds(hidden_chunk * (c - 4), hidden_chunk), :]
        return qkv_buf.at[{3: 2, 6: 0, 7: 1}[c], pl.ds(0, hidden_chunk), :]

    def down_copy(c):
        return pltpu.make_async_copy(
            down_ref.at[pl.ds(hidden_chunk * c, hidden_chunk), :], down_place(c), down_sems.at[c]
        )

    def remote(src, dst, send, recv):
        return pltpu.make_async_remote_copy(
            src_ref=src, dst_ref=dst, send_sem=send, recv_sem=recv, device_id=partner, device_id_type=MESH
        )

    x_copy = pltpu.make_async_copy(x_ref, x_t, x_sem)
    small = [
        pltpu.make_async_copy(src, dst, small_sems.at[k])
        for k, (src, dst) in enumerate(
            ((gains_hbm, gains_ref), (segment_hbm, segment_ref), (owner_hbm, owner_ref))
        )
    ]
    x_copy.start()
    for copy in small:
        copy.start()
    for s in range(3):
        qkv_copy(s).start()
    for h in range(head_count):
        wout_copy(h).start()

    barrier = pltpu.get_barrier_semaphore()
    for peer in place.others():
        pl.semaphore_signal(barrier, inc=1, device_id={"req": peer}, device_id_type=MESH)
    pl.semaphore_signal(barrier, inc=1, device_id=partner, device_id_type=MESH)

    for copy in small:
        copy.wait()
    for j in range(2):
        own_rows[j] = jnp.full((1, 128), owner_ref[j], jnp.int32)
    for h in range(head_count):
        wout_buf[pl.ds(128 * h + HEAD_DIM, 128 - HEAD_DIM), :] = jnp.zeros((128 - HEAD_DIM, width), bf16)
        for s in range(3):
            heads[s, h, pl.ds(HEAD_DIM, 128 - HEAD_DIM), :] = jnp.zeros((128 - HEAD_DIM, count), bf16)
    seg_rows = jnp.broadcast_to(segment_ref[...], (count, count))
    same = seg_rows == seg_rows.T

    x_copy.wait()
    total = jnp.zeros((1, count), f32)
    for b in range(width // 128):
        total += jnp.sum(x_t[pl.ds(128 * b, 128), :].astype(f32), axis=0, keepdims=True)
    mean = total * (1.0 / width)
    total = jnp.zeros((1, count), f32)
    for b in range(width // 128):
        center = x_t[pl.ds(128 * b, 128), :].astype(f32) - mean
        total += jnp.sum(center * center, axis=0, keepdims=True)
    scale = lax.rsqrt(total * (1.0 / width) + 1e-06)
    for b in range(width // 128):
        gain = jnp.broadcast_to(gains_ref[0:1, pl.ds(128 * b, 128)], (128, 128)).T
        gain = jnp.concatenate([gain] * (count // 128), axis=1)
        x = x_t[pl.ds(128 * b, 128), :].astype(f32)
        normed_t[pl.ds(128 * b, 128), :] = ((x - mean) * scale * gain).astype(bf16)

    for s in range(3):
        qkv_copy(s).wait()
        for c in range(2 * s, min(2 * s + 2, middle)):
            up_copy(c).start()
            if c < 3:
                down_copy(c).start()
        product = jnp.dot(qkv_buf[s], normed_t[...], preferred_element_type=f32)
        for h in range(head_count):
            heads[s, h, pl.ds(0, HEAD_DIM), :] = product[HEAD_DIM * h : HEAD_DIM * (h + 1)].astype(bf16)
    down_copy(3).start()

    for h in range(head_count):
        keys = heads[1, h].T
        for start in range(0, count, 128):
            queries = pl.ds(start, 128)
            scores = jnp.dot(keys, heads[0, h, :, queries], preferred_element_type=f32)
            scores = jnp.where(same[:, start : start + 128], scores * HEAD_DIM ** (-0.5), -1e30)
            top = jnp.max(scores, axis=0, keepdims=True)
            expo = jnp.exp(scores - top)
            share = 1.0 / jnp.sum(expo, axis=0, keepdims=True)
            mixed = jnp.dot(heads[2, h], expo.astype(bf16), preferred_element_type=f32) * share
            context[queries, pl.ds(128 * h, 128)] = mixed.T.astype(bf16)

    for h in range(head_count):
        wout_copy(h).wait()
    pl.semaphore_wait(barrier, 64)
    swaps = []
    for k, (start, size) in enumerate(cuts):
        cols = pl.ds(start, size)
        product = jnp.dot(context[...], wout_buf[:, cols], preferred_element_type=f32)
        sent[:, cols] = product.astype(bf16)
        swap = remote(sent.at[:, cols], got1.at[:, cols], s1_sems.at[k], r1_sems.at[k])
        swap.start()
        swaps.append(swap)
        resid[:, cols] = product + x_t[cols, :].astype(f32).T

    for c in range(middle, hidden_chunks):
        up_copy(c).start()
        down_copy(c).start()

    for peer in place.others():
        pltpu.make_async_remote_copy(
            src_ref=own_rows.at[peer // 32], dst_ref=table.at[me], send_sem=send_sem_o, recv_sem=recv_sem_o,
            device_id={"req": peer}, device_id_type=MESH,
        ).start()
    table[me] = own_rows[me // 32]

    for swap in swaps:
        swap.wait()

    def norm_to(which, out, extra):
        for b in range(count // 32):
            rows = pl.ds(32 * b, 32)
            x = resid[rows, :] + extra[rows, :].astype(f32)
            resid[rows, :] = x
            center = x - jnp.sum(x, axis=1, keepdims=True) * (1.0 / width)
            spread = jnp.sum(center * center, axis=1, keepdims=True) * (1.0 / width)
            out[rows, :] = (center * lax.rsqrt(spread + 1e-06) * gains_ref[which : which + 1, :]).astype(bf16)

    norm_to(1, normed, got1)

    def up(c, out):
        out[...] = jnp.dot(normed[...], pool[c], preferred_element_type=f32)

    def gelu(pre, out):
        u = pre[...]
        out[...] = (0.5 * u * (1.0 + lax.erf(u * 0.5**0.5))).astype(bf16)

    def down(c, hid):
        product = jnp.dot(hid[...], down_place(c)[...], preferred_element_type=f32)
        acc[...] = product if c == 0 else acc[...] + product

    def wait_chunks(chunks):
        for c in chunks:
            up_copy(c).wait()
            down_copy(c).wait()

    wait_chunks(range(middle))
    for m in range(spare):
        merge_copy(m).start()
    up(0, pre_a)
    up(1, pre_b)
    gelu(pre_a, hid_a)
    for c in range(0, hidden_chunks - 2, 2):
        if c + 2 == middle:
            wait_chunks(range(middle, hidden_chunks))
            for m in range(middle):
                merge_copy(spare + m).start()
        up(c + 2, pre_a)
        gelu(pre_b, hid_b)
        down(c, hid_a)
        up(c + 3, pre_b)
        gelu(pre_a, hid_a)
        down(c + 1, hid_b)

    gelu(pre_b, hid_b)
    down(hidden_chunks - 2, hid_a)
    swaps = []
    for k, (start, size) in enumerate(cuts):
        cols = pl.ds(start, size)
        product = acc[:, cols] + jnp.dot(
            hid_b[...], down_place(hidden_chunks - 1)[:, cols], preferred_element_type=f32
        )
        sent[:, cols] = product.astype(bf16)
        swap = remote(sent.at[:, cols], got2.at[:, cols], s2_sems.at[k], r2_sems.at[k])
        swap.start()
        swaps.append(swap)
        resid[:, cols] += product
    for m in range(middle, hidden_chunks):
        merge_copy(spare + m).start()

    row = lax.broadcasted_iota(jnp.int32, (count, count), 0)
    token = lax.broadcasted_iota(jnp.int32, (count, count), 1)
    quarter = count // 4
    part, request, rank = row // quarter, lax.rem(row, quarter) // CAP, lax.rem(row, CAP)
    first = jnp.sum((segment_ref[...] < 1).astype(jnp.int32), axis=1, keepdims=True)
    want = request * first + 4 * rank + part
    pick = jnp.where((token == want) & (segment_ref[...] == request), 1.0, 0.0).astype(bf16)

    def all_but_one(ref):
        return ref.at[pl.ds(0, 63)]

    def wait_all(ref, sem):
        pltpu.make_async_copy(all_but_one(ref), all_but_one(ref), sem).wait()

    wait_all(table, recv_sem_o)
    lanes = lax.broadcasted_iota(jnp.int32, (64, 1, 128), 2)
    sources = lax.broadcasted_iota(jnp.int32, (64, 1, 128), 0)
    inv_v[...] = jnp.max(jnp.where(table[...] == lanes, sources, 0), axis=0)
    to_scalar = pltpu.make_async_copy(inv_v, inv_s, inv_sem)
    to_scalar.start()
    to_scalar.wait()

    for swap in swaps:
        swap.wait()
    norm_to(2, normed, got2)
    for i in range(4):
        merged[:, pl.ds(width * i, width)] = jnp.dot(
            pick[quarter * i : quarter * (i + 1)], normed[...], preferred_element_type=f32
        ).astype(bf16)

    for k, dy in enumerate((2, 3, 1, 0)):
        for i in range(4):
            merge_copy(4 * k + i).wait()
        product = jnp.zeros((quarter, hidden_chunk), f32)
        for i in range(4):
            m = 4 * k + i
            product += jnp.dot(
                merged[:, pl.ds(width * i, width)], pool[(hidden_chunks + m) % slots], preferred_element_type=f32
            )
        for g in range(4):
            for x in range(4):
                tiles[g * 16 + place.y[dy] * 4 + x] = product[16 * g : 16 * g + 16, 128 * x : 128 * x + 128].astype(bf16)
        for peer in place.others((dy,)):
            pltpu.make_async_remote_copy(
                src_ref=tiles.at[peer], dst_ref=inbox.at[me], send_sem=send_sem_a, recv_sem=recv_sem_a,
                device_id={"req": peer}, device_id_type=MESH,
            ).start()
    inbox[me] = tiles[me]
    wait_all(inbox, recv_sem_a)

    for d in range(64):
        sorted_tiles[d] = inbox[inv_s[0, d]]
    for peer in place.others():
        pltpu.make_async_remote_copy(
            src_ref=sorted_tiles.at[peer], dst_ref=landed.at[me], send_sem=send_sem_b, recv_sem=recv_sem_b,
            device_id={"req": peer}, device_id_type=MESH,
        ).start()
    landed[me] = sorted_tiles[me]
    wait_all(landed, recv_sem_b)
    for g in range(4):
        for c in range(16):
            out_ref[pl.ds(16 * g, 16), pl.ds(128 * c, 128)] = landed[g * 16 + c]
    wait_all(table, send_sem_o)
    wait_all(tiles, send_sem_a)
    wait_all(sorted_tiles, send_sem_b)


def layer(x_t, segment, owner, qkv_t, w_out, w_up, w_down, gains, w_merge):
    width, count = x_t.shape
    half = width // 2
    hidden = w_up.shape[1]
    chunk = 512
    chunks = hidden // chunk
    slots = 16
    heads = half // HEAD_DIM
    rows, out_width = count // 4, w_merge.shape[1]
    f32, bf16 = jnp.float32, jnp.bfloat16
    vmem = pl.BlockSpec(memory_space=pltpu.VMEM)
    hbm = pl.BlockSpec(memory_space=pltpu.HBM)
    dma = pltpu.SemaphoreType.DMA
    return pl.pallas_call(
        layer_kernel,
        out_shape=jax.ShapeDtypeStruct((rows, out_width), bf16),
        in_specs=[hbm] * 9,
        out_specs=vmem,
        scratch_shapes=[
            pltpu.VMEM((width, count), bf16),
            pltpu.VMEM((1, count), jnp.int32),
            pltpu.SMEM((2,), jnp.int32),
            pltpu.VMEM((3, width), f32),
            pltpu.VMEM((3, half, width), bf16),
            pltpu.VMEM((heads * 128, width), bf16),
            pltpu.VMEM((slots, width, chunk), bf16),
            pltpu.VMEM((3, chunk, width), bf16),
            pltpu.VMEM((width, count), bf16),
            pltpu.VMEM((3, heads, 128, count), bf16),
            pltpu.VMEM((count, heads * 128), bf16),
            pltpu.VMEM((count, width), f32),
            pltpu.VMEM((count, width), f32),
            pltpu.VMEM((count, width), bf16),
            pltpu.VMEM((count, chunk), f32),
            pltpu.VMEM((count, chunk), f32),
            pltpu.VMEM((count, chunk), bf16),
            pltpu.VMEM((count, chunk), bf16),
        ]
        + [pltpu.VMEM((count, width), bf16)] * 3
        + [pltpu.VMEM((rows, 4 * width), bf16)]
        + [pltpu.VMEM((64, 16, 128), bf16)] * 4
        + [
            pltpu.VMEM((2, 1, 128), jnp.int32),
            pltpu.VMEM((64, 1, 128), jnp.int32),
            pltpu.VMEM((1, 128), jnp.int32),
            pltpu.SMEM((1, 128), jnp.int32),
        ]
        + [dma, dma((3,)), dma((3,)), dma((heads,)), dma((slots,)), dma((chunks,))]
        + [dma((3,))] * 4
        + [dma] * 7,
        compiler_params=pltpu.CompilerParams(
            collective_id=2, has_side_effects=True, vmem_limit_bytes=62 * 1024 * 1024
        ),
        name="layer",
    )(x_t, segment, owner, qkv_t, w_out, w_up, w_down, gains, w_merge)


def local(patches, segment, owner, w_qkv, w_out, w_up, w_down, gains, w_merge):
    x_t = swap_halves(patches.T)
    return layer(
        x_t, segment.reshape(1, -1), owner, w_qkv.transpose(0, 2, 1), w_out, w_up, w_down, gains, w_merge
    )


def solution(mesh):
    in_specs = (
        P("req", "tp"),
        P("req"),
        P("req"),
        P(None, None, "tp"),
        P("tp", None),
        P(None, "tp"),
        P("tp", None),
        P(),
        P(None, "tp"),
    )
    out_specs = P("req", "tp")
    return jax.shard_map(local, mesh=mesh, in_specs=in_specs, out_specs=out_specs, check_vma=False)
```

```python
import functools

import jax
import jax.numpy as jnp
from jax import lax
from jax.experimental import pallas as pl
from jax.experimental.pallas import tpu as pltpu
from jax.sharding import PartitionSpec as P

HEAD_DIM = 104
CAP = 32
MESH = pl.DeviceIdType.MESH


class Place:
    def __init__(self):
        self.me = lax.axis_index("req")
        x, y, z = lax.rem(self.me, 4), lax.rem(self.me // 4, 4), self.me // 16
        self.x = [lax.rem(x + k, 4) for k in range(4)]
        self.y = [lax.rem(y + k, 4) for k in range(4)]
        self.z = [lax.rem(z + k, 4) for k in range(4)]

    def peer(self, dz, dy, dx):
        return self.z[dz] * 16 + self.y[dy] * 4 + self.x[dx]

    def others(self, dys=(2, 3, 1, 0)):
        for dy in dys:
            for dz in (2, 3, 1, 0):
                for dx in (2, 3, 1, 0):
                    if (dz, dy, dx) != (0, 0, 0):
                        yield self.peer(dz, dy, dx)


def swap_kernel(patches_ref, out_ref, send_sem, recv_sem):
    partner = {"tp": 1 - lax.axis_index("tp")}
    barrier = pltpu.get_barrier_semaphore()
    pl.semaphore_signal(barrier, inc=1, device_id=partner, device_id_type=MESH)
    pl.semaphore_wait(barrier, 1)
    swap = pltpu.make_async_remote_copy(
        src_ref=patches_ref, dst_ref=out_ref, send_sem=send_sem, recv_sem=recv_sem,
        device_id=partner, device_id_type=MESH,
    )
    swap.start()
    swap.wait()


def swap_halves(patches_t):
    dma = pltpu.SemaphoreType.DMA
    hbm = pl.BlockSpec(memory_space=pltpu.HBM)
    return pl.pallas_call(
        swap_kernel,
        out_shape=jax.ShapeDtypeStruct(patches_t.shape, patches_t.dtype),
        in_specs=[hbm],
        out_specs=hbm,
        scratch_shapes=[dma, dma],
        compiler_params=pltpu.CompilerParams(
            collective_id=1, has_side_effects=True, vmem_limit_bytes=62 * 1024 * 1024
        ),
        name="swap_halves",
    )(patches_t)


def layer_kernel(
    own_ref, other_ref, segment_hbm, owner_hbm, qkv_ref, wout_ref, up_ref, down_ref, gains_hbm, merge_ref, out_ref,
    x_t, segment_ref, owner_ref, gains_ref, qkv_buf, wout_buf, pool, down_buf, normed_t, heads, context, resid, acc, normed,
    pre_a, pre_b, hid_a, hid_b, sent, got1, got2,
    merged, tiles, inbox, sorted_tiles, landed, own_rows, table, inv_v, inv_s,
    x_sems, small_sems, qkv_sems, wout_sems, pool_sems, down_sems, s1_sems, r1_sems, s2_sems, r2_sems,
    send_sem_o, recv_sem_o, inv_sem, send_sem_a, recv_sem_a, send_sem_b, recv_sem_b,
):
    f32, bf16 = jnp.float32, jnp.bfloat16
    tp = lax.axis_index("tp")
    partner = {"tp": 1 - tp}
    place = Place()
    me = place.me
    width, count = x_t.shape
    half = width // 2
    head_count = half // HEAD_DIM
    slots, _, hidden_chunk = pool.shape
    hidden_chunks = down_ref.shape[0] // hidden_chunk
    middle = hidden_chunks // 2
    spare = slots - hidden_chunks
    cuts = [(0, 640), (640, 512), (1152, 512)]

    def qkv_copy(s):
        return pltpu.make_async_copy(qkv_ref.at[s], qkv_buf.at[s], qkv_sems.at[s])

    def wout_copy(h):
        return pltpu.make_async_copy(
            wout_ref.at[pl.ds(HEAD_DIM * h, HEAD_DIM), :], wout_buf.at[pl.ds(128 * h, HEAD_DIM), :], wout_sems.at[h]
        )

    def up_copy(c):
        return pltpu.make_async_copy(
            up_ref.at[:, pl.ds(hidden_chunk * c, hidden_chunk)], pool.at[c], pool_sems.at[c]
        )

    def merge_cols(m):
        return pl.ds(pl.multiple_of(place.y[(2, 3, 1, 0)[m // 4]] * hidden_chunk, hidden_chunk), hidden_chunk)

    def merge_copy(m):
        slot = (hidden_chunks + m) % slots
        return pltpu.make_async_copy(
            merge_ref.at[pl.ds(width * (m % 4), width), merge_cols(m)], pool.at[slot], pool_sems.at[slot]
        )

    def down_place(c):
        if c < 3:
            return down_buf.at[c]
        if c in (4, 5):
            return wout_buf.at[pl.ds(hidden_chunk * (c - 4), hidden_chunk), :]
        return qkv_buf.at[{3: 2, 6: 0, 7: 1}[c], pl.ds(0, hidden_chunk), :]

    def down_copy(c):
        return pltpu.make_async_copy(
            down_ref.at[pl.ds(hidden_chunk * c, hidden_chunk), :], down_place(c), down_sems.at[c]
        )

    def remote(src, dst, send, recv):
        return pltpu.make_async_remote_copy(
            src_ref=src, dst_ref=dst, send_sem=send, recv_sem=recv, device_id=partner, device_id_type=MESH
        )

    x_copies = [
        pltpu.make_async_copy(src, x_t.at[pl.ds(side * half, half), :], x_sems.at[k])
        for k, (src, side) in enumerate(((own_ref, tp), (other_ref, 1 - tp)))
    ]
    small = [
        pltpu.make_async_copy(src, dst, small_sems.at[k])
        for k, (src, dst) in enumerate(
            ((gains_hbm, gains_ref), (segment_hbm, segment_ref), (owner_hbm, owner_ref))
        )
    ]
    for copy in x_copies:
        copy.start()
    for copy in small:
        copy.start()
    for s in range(3):
        qkv_copy(s).start()
    for h in range(head_count):
        wout_copy(h).start()

    barrier = pltpu.get_barrier_semaphore()
    for peer in place.others():
        pl.semaphore_signal(barrier, inc=1, device_id={"req": peer}, device_id_type=MESH)
    pl.semaphore_signal(barrier, inc=1, device_id=partner, device_id_type=MESH)

    for copy in small:
        copy.wait()
    for j in range(2):
        own_rows[j] = jnp.full((1, 128), owner_ref[j], jnp.int32)
    for h in range(head_count):
        wout_buf[pl.ds(128 * h + HEAD_DIM, 128 - HEAD_DIM), :] = jnp.zeros((128 - HEAD_DIM, width), bf16)
        for s in range(3):
            heads[s, h, pl.ds(HEAD_DIM, 128 - HEAD_DIM), :] = jnp.zeros((128 - HEAD_DIM, count), bf16)
    seg_rows = jnp.broadcast_to(segment_ref[...], (count, count))
    same = pre_a.at[:, pl.ds(0, count)]
    same[...] = jnp.where(seg_rows == seg_rows.T, 0.0, -1e30)

    for copy in x_copies:
        copy.wait()
    total = jnp.zeros((1, count), f32)
    for b in range(width // 128):
        total += jnp.sum(x_t[pl.ds(128 * b, 128), :].astype(f32), axis=0, keepdims=True)
    mean = total * (1.0 / width)
    total = jnp.zeros((1, count), f32)
    for b in range(width // 128):
        center = x_t[pl.ds(128 * b, 128), :].astype(f32) - mean
        total += jnp.sum(center * center, axis=0, keepdims=True)
    scale = lax.rsqrt(total * (1.0 / width) + 1e-06)
    for b in range(width // 128):
        gain = jnp.broadcast_to(gains_ref[0:1, pl.ds(128 * b, 128)], (128, 128)).T
        gain = jnp.concatenate([gain] * (count // 128), axis=1)
        x = x_t[pl.ds(128 * b, 128), :].astype(f32)
        normed_t[pl.ds(128 * b, 128), :] = ((x - mean) * scale * gain).astype(bf16)

    for s in range(3):
        qkv_copy(s).wait()
        for c in range(2 * s, min(2 * s + 2, middle)):
            up_copy(c).start()
            if c < 3:
                down_copy(c).start()
        product = jnp.dot(qkv_buf[s], normed_t[...], preferred_element_type=f32)
        for h in range(head_count):
            heads[s, h, pl.ds(0, HEAD_DIM), :] = product[HEAD_DIM * h : HEAD_DIM * (h + 1)].astype(bf16)
    down_copy(3).start()

    for h in range(head_count):
        scores = lax.dot_general(
            heads[1, h], heads[0, h], (((0,), (0,)), ((), ())), preferred_element_type=f32
        )
        scores = jnp.where(same[...] == 0.0, scores * HEAD_DIM ** (-0.5), -1e30)
        top = jnp.max(scores, axis=0, keepdims=True)
        expo = jnp.exp(scores - top)
        share = 1.0 / jnp.sum(expo, axis=0, keepdims=True)
        mixed = jnp.dot(heads[2, h], expo.astype(bf16), preferred_element_type=f32) * share
        context[:, pl.ds(128 * h, 128)] = mixed.T.astype(bf16)

    for h in range(head_count):
        wout_copy(h).wait()
    pl.semaphore_wait(barrier, 64)
    swaps = []
    for k, (start, size) in enumerate(cuts):
        cols = pl.ds(start, size)
        product = jnp.dot(context[...], wout_buf[:, cols], preferred_element_type=f32)
        sent[:, cols] = product.astype(bf16)
        swap = remote(sent.at[:, cols], got1.at[:, cols], s1_sems.at[k], r1_sems.at[k])
        swap.start()
        swaps.append(swap)
        resid[:, cols] = product + x_t[cols, :].astype(f32).T

    for c in range(middle, hidden_chunks):
        up_copy(c).start()
        down_copy(c).start()

    for peer in place.others():
        pltpu.make_async_remote_copy(
            src_ref=own_rows.at[peer // 32], dst_ref=table.at[me], send_sem=send_sem_o, recv_sem=recv_sem_o,
            device_id={"req": peer}, device_id_type=MESH,
        ).start()
    table[me] = own_rows[me // 32]

    for swap in swaps:
        swap.wait()

    def norm_to(which, out, extra):
        for b in range(count // 32):
            rows = pl.ds(32 * b, 32)
            x = resid[rows, :] + extra[rows, :].astype(f32)
            resid[rows, :] = x
            center = x - jnp.sum(x, axis=1, keepdims=True) * (1.0 / width)
            spread = jnp.sum(center * center, axis=1, keepdims=True) * (1.0 / width)
            out[rows, :] = (center * lax.rsqrt(spread + 1e-06) * gains_ref[which : which + 1, :]).astype(bf16)

    norm_to(1, normed, got1)

    def up(c, out):
        out[...] = jnp.dot(normed[...], pool[c], preferred_element_type=f32)

    def gelu(pre, out):
        u = pre[...]
        out[...] = (0.5 * u * (1.0 + lax.erf(u * 0.5**0.5))).astype(bf16)

    def down(c, hid):
        product = jnp.dot(hid[...], down_place(c)[...], preferred_element_type=f32)
        acc[...] = product if c == 0 else acc[...] + product

    def wait_chunks(chunks):
        for c in chunks:
            up_copy(c).wait()
            down_copy(c).wait()

    wait_chunks(range(middle))
    for m in range(spare):
        merge_copy(m).start()
    up(0, pre_a)
    up(1, pre_b)
    gelu(pre_a, hid_a)
    for c in range(0, hidden_chunks - 2, 2):
        if c + 2 == middle:
            wait_chunks(range(middle, hidden_chunks))
            for m in range(middle):
                merge_copy(spare + m).start()
        up(c + 2, pre_a)
        gelu(pre_b, hid_b)
        down(c, hid_a)
        up(c + 3, pre_b)
        gelu(pre_a, hid_a)
        down(c + 1, hid_b)

    gelu(pre_b, hid_b)
    down(hidden_chunks - 2, hid_a)
    swaps = []
    for k, (start, size) in enumerate(cuts):
        cols = pl.ds(start, size)
        product = acc[:, cols] + jnp.dot(
            hid_b[...], down_place(hidden_chunks - 1)[:, cols], preferred_element_type=f32
        )
        sent[:, cols] = product.astype(bf16)
        swap = remote(sent.at[:, cols], got2.at[:, cols], s2_sems.at[k], r2_sems.at[k])
        swap.start()
        swaps.append(swap)
        resid[:, cols] += product
    for m in range(middle, hidden_chunks):
        merge_copy(spare + m).start()

    row = lax.broadcasted_iota(jnp.int32, (count, count), 0)
    token = lax.broadcasted_iota(jnp.int32, (count, count), 1)
    quarter = count // 4
    part, request, rank = row // quarter, lax.rem(row, quarter) // CAP, lax.rem(row, CAP)
    first = jnp.sum((segment_ref[...] < 1).astype(jnp.int32), axis=1, keepdims=True)
    want = request * first + 4 * rank + part
    pick = jnp.where((token == want) & (segment_ref[...] == request), 1.0, 0.0).astype(bf16)

    def all_but_one(ref):
        return ref.at[pl.ds(0, 63)]

    def wait_all(ref, sem):
        pltpu.make_async_copy(all_but_one(ref), all_but_one(ref), sem).wait()

    wait_all(table, recv_sem_o)
    lanes = lax.broadcasted_iota(jnp.int32, (64, 1, 128), 2)
    sources = lax.broadcasted_iota(jnp.int32, (64, 1, 128), 0)
    inv_v[...] = jnp.max(jnp.where(table[...] == lanes, sources, 0), axis=0)
    to_scalar = pltpu.make_async_copy(inv_v, inv_s, inv_sem)
    to_scalar.start()
    to_scalar.wait()

    for swap in swaps:
        swap.wait()
    norm_to(2, normed, got2)
    for i in range(4):
        merged[:, pl.ds(width * i, width)] = jnp.dot(
            pick[quarter * i : quarter * (i + 1)], normed[...], preferred_element_type=f32
        ).astype(bf16)

    for k, dy in enumerate((2, 3, 1, 0)):
        for i in range(4):
            merge_copy(4 * k + i).wait()
        product = jnp.zeros((quarter, hidden_chunk), f32)
        for i in range(4):
            m = 4 * k + i
            product += jnp.dot(
                merged[:, pl.ds(width * i, width)], pool[(hidden_chunks + m) % slots], preferred_element_type=f32
            )
        for g in range(4):
            for x in range(4):
                tiles[g * 16 + place.y[dy] * 4 + x] = product[16 * g : 16 * g + 16, 128 * x : 128 * x + 128].astype(bf16)
        for peer in place.others((dy,)):
            pltpu.make_async_remote_copy(
                src_ref=tiles.at[peer], dst_ref=inbox.at[me], send_sem=send_sem_a, recv_sem=recv_sem_a,
                device_id={"req": peer}, device_id_type=MESH,
            ).start()
    inbox[me] = tiles[me]
    wait_all(inbox, recv_sem_a)

    for d in range(64):
        sorted_tiles[d] = inbox[inv_s[0, d]]
    for peer in place.others():
        pltpu.make_async_remote_copy(
            src_ref=sorted_tiles.at[peer], dst_ref=landed.at[me], send_sem=send_sem_b, recv_sem=recv_sem_b,
            device_id={"req": peer}, device_id_type=MESH,
        ).start()
    landed[me] = sorted_tiles[me]
    wait_all(landed, recv_sem_b)
    for g in range(4):
        for c in range(16):
            out_ref[pl.ds(16 * g, 16), pl.ds(128 * c, 128)] = landed[g * 16 + c]
    wait_all(table, send_sem_o)
    wait_all(tiles, send_sem_a)
    wait_all(sorted_tiles, send_sem_b)


def layer(own, other, segment, owner, qkv_t, w_out, w_up, w_down, gains, w_merge):
    half, count = own.shape
    width = 2 * half
    hidden = w_up.shape[1]
    chunk = 512
    chunks = hidden // chunk
    slots = 16
    heads = half // HEAD_DIM
    rows, out_width = count // 4, w_merge.shape[1]
    f32, bf16 = jnp.float32, jnp.bfloat16
    vmem = pl.BlockSpec(memory_space=pltpu.VMEM)
    hbm = pl.BlockSpec(memory_space=pltpu.HBM)
    dma = pltpu.SemaphoreType.DMA
    return pl.pallas_call(
        layer_kernel,
        out_shape=jax.ShapeDtypeStruct((rows, out_width), bf16),
        in_specs=[hbm] * 10,
        out_specs=vmem,
        scratch_shapes=[
            pltpu.VMEM((width, count), bf16),
            pltpu.VMEM((1, count), jnp.int32),
            pltpu.SMEM((2,), jnp.int32),
            pltpu.VMEM((3, width), f32),
            pltpu.VMEM((3, half, width), bf16),
            pltpu.VMEM((heads * 128, width), bf16),
            pltpu.VMEM((slots, width, chunk), bf16),
            pltpu.VMEM((3, chunk, width), bf16),
            pltpu.VMEM((width, count), bf16),
            pltpu.VMEM((3, heads, 128, count), bf16),
            pltpu.VMEM((count, heads * 128), bf16),
            pltpu.VMEM((count, width), f32),
            pltpu.VMEM((count, width), f32),
            pltpu.VMEM((count, width), bf16),
            pltpu.VMEM((count, chunk), f32),
            pltpu.VMEM((count, chunk), f32),
            pltpu.VMEM((count, chunk), bf16),
            pltpu.VMEM((count, chunk), bf16),
        ]
        + [pltpu.VMEM((count, width), bf16)] * 3
        + [pltpu.VMEM((rows, 4 * width), bf16)]
        + [pltpu.VMEM((64, 16, 128), bf16)] * 4
        + [
            pltpu.VMEM((2, 1, 128), jnp.int32),
            pltpu.VMEM((64, 1, 128), jnp.int32),
            pltpu.VMEM((1, 128), jnp.int32),
            pltpu.SMEM((1, 128), jnp.int32),
        ]
        + [dma((2,)), dma((3,)), dma((3,)), dma((heads,)), dma((slots,)), dma((chunks,))]
        + [dma((3,))] * 4
        + [dma] * 7,
        compiler_params=pltpu.CompilerParams(
            collective_id=2, has_side_effects=True, vmem_limit_bytes=62 * 1024 * 1024
        ),
        name="layer",
    )(own, other, segment, owner, qkv_t, w_out, w_up, w_down, gains, w_merge)


def local(patches, segment, owner, w_qkv, w_out, w_up, w_down, gains, w_merge):
    own = patches.T
    return layer(
        own, swap_halves(own), segment.reshape(1, -1), owner, w_qkv.transpose(0, 2, 1), w_out, w_up, w_down,
        gains, w_merge,
    )


def solution(mesh):
    in_specs = (
        P("req", "tp"),
        P("req"),
        P("req"),
        P(None, None, "tp"),
        P("tp", None),
        P(None, "tp"),
        P("tp", None),
        P(),
        P(None, "tp"),
    )
    out_specs = P("req", "tp")
    return jax.shard_map(local, mesh=mesh, in_specs=in_specs, out_specs=out_specs, check_vma=False)
```

```python
import functools

import jax
import jax.numpy as jnp
from jax import lax
from jax.experimental import pallas as pl
from jax.experimental.pallas import tpu as pltpu
from jax.sharding import PartitionSpec as P

HEAD_DIM = 104
CAP = 32
MESH = pl.DeviceIdType.MESH


class Place:
    def __init__(self):
        self.me = lax.axis_index("req")
        x, y, z = lax.rem(self.me, 4), lax.rem(self.me // 4, 4), self.me // 16
        self.x = [lax.rem(x + k, 4) for k in range(4)]
        self.y = [lax.rem(y + k, 4) for k in range(4)]
        self.z = [lax.rem(z + k, 4) for k in range(4)]

    def peer(self, dz, dy, dx):
        return self.z[dz] * 16 + self.y[dy] * 4 + self.x[dx]

    def others(self, dys=(2, 3, 1, 0)):
        for dy in dys:
            for dz in (2, 3, 1, 0):
                for dx in (2, 3, 1, 0):
                    if (dz, dy, dx) != (0, 0, 0):
                        yield self.peer(dz, dy, dx)


def swap_kernel(patches_ref, out_ref, send_sem, recv_sem):
    partner = {"tp": 1 - lax.axis_index("tp")}
    barrier = pltpu.get_barrier_semaphore()
    pl.semaphore_signal(barrier, inc=1, device_id=partner, device_id_type=MESH)
    pl.semaphore_wait(barrier, 1)
    swap = pltpu.make_async_remote_copy(
        src_ref=patches_ref, dst_ref=out_ref, send_sem=send_sem, recv_sem=recv_sem,
        device_id=partner, device_id_type=MESH,
    )
    swap.start()
    swap.wait()


def swap_halves(patches_t):
    dma = pltpu.SemaphoreType.DMA
    hbm = pl.BlockSpec(memory_space=pltpu.HBM)
    return pl.pallas_call(
        swap_kernel,
        out_shape=jax.ShapeDtypeStruct(patches_t.shape, patches_t.dtype),
        in_specs=[hbm],
        out_specs=hbm,
        scratch_shapes=[dma, dma],
        compiler_params=pltpu.CompilerParams(
            collective_id=1, has_side_effects=True, vmem_limit_bytes=62 * 1024 * 1024
        ),
        name="swap_halves",
    )(patches_t)


def layer_kernel(
    own_ref, other_ref, segment_hbm, owner_hbm, qkv_ref, wout_ref, up_ref, down_ref, gains_hbm, merge_ref, out_ref,
    x_t, segment_ref, owner_ref, gains_ref, qkv_buf, wout_buf, pool, down_buf, normed_t, heads, context, resid, acc, normed,
    pre_a, pre_b, hid_a, hid_b, sent, got1, got2,
    merged, tiles, inbox, sorted_tiles, landed, own_rows, table, inv_v, inv_s,
    x_sems, small_sems, qkv_sems, wout_sems, pool_sems, down_sems, s1_sems, r1_sems, s2_sems, r2_sems,
    send_sem_o, recv_sem_o, inv_sem, send_sem_a, recv_sem_a, send_sem_b, recv_sem_b,
):
    f32, bf16 = jnp.float32, jnp.bfloat16
    tp = lax.axis_index("tp")
    partner = {"tp": 1 - tp}
    place = Place()
    me = place.me
    width, count = x_t.shape
    half = width // 2
    head_count = half // HEAD_DIM
    slots, _, hidden_chunk = pool.shape
    hidden_chunks = down_ref.shape[0] // hidden_chunk
    middle = hidden_chunks // 2
    spare = slots - hidden_chunks
    cuts = [(0, 640), (640, 512), (1152, 512)]

    def qkv_copy(s):
        return pltpu.make_async_copy(qkv_ref.at[s], qkv_buf.at[s], qkv_sems.at[s])

    def wout_copy(h):
        return pltpu.make_async_copy(
            wout_ref.at[pl.ds(HEAD_DIM * h, HEAD_DIM), :], wout_buf.at[pl.ds(128 * h, HEAD_DIM), :], wout_sems.at[h]
        )

    def up_copy(c):
        return pltpu.make_async_copy(
            up_ref.at[:, pl.ds(hidden_chunk * c, hidden_chunk)], pool.at[c], pool_sems.at[c]
        )

    def merge_cols(m):
        return pl.ds(pl.multiple_of(place.y[(2, 3, 1, 0)[m // 4]] * hidden_chunk, hidden_chunk), hidden_chunk)

    def merge_copy(m):
        slot = (hidden_chunks + m) % slots
        return pltpu.make_async_copy(
            merge_ref.at[pl.ds(width * (m % 4), width), merge_cols(m)], pool.at[slot], pool_sems.at[slot]
        )

    def down_place(c):
        if c < 3:
            return down_buf.at[c]
        if c in (4, 5):
            return wout_buf.at[pl.ds(hidden_chunk * (c - 4), hidden_chunk), :]
        return qkv_buf.at[{3: 2, 6: 0, 7: 1}[c], pl.ds(0, hidden_chunk), :]

    def down_copy(c):
        return pltpu.make_async_copy(
            down_ref.at[pl.ds(hidden_chunk * c, hidden_chunk), :], down_place(c), down_sems.at[c]
        )

    def remote(src, dst, send, recv):
        return pltpu.make_async_remote_copy(
            src_ref=src, dst_ref=dst, send_sem=send, recv_sem=recv, device_id=partner, device_id_type=MESH
        )

    x_copies = [
        pltpu.make_async_copy(src, x_t.at[pl.ds(side * half, half), :], x_sems.at[k])
        for k, (src, side) in enumerate(((own_ref, tp), (other_ref, 1 - tp)))
    ]
    small = [
        pltpu.make_async_copy(src, dst, small_sems.at[k])
        for k, (src, dst) in enumerate(
            ((gains_hbm, gains_ref), (segment_hbm, segment_ref), (owner_hbm, owner_ref))
        )
    ]
    for copy in x_copies:
        copy.start()
    for copy in small:
        copy.start()
    for s in range(3):
        qkv_copy(s).start()
    for h in range(head_count):
        wout_copy(h).start()

    barrier = pltpu.get_barrier_semaphore()
    for peer in place.others():
        pl.semaphore_signal(barrier, inc=1, device_id={"req": peer}, device_id_type=MESH)
    pl.semaphore_signal(barrier, inc=1, device_id=partner, device_id_type=MESH)

    for copy in small:
        copy.wait()
    for j in range(2):
        own_rows[j] = jnp.full((1, 128), owner_ref[j], jnp.int32)
    for h in range(head_count):
        wout_buf[pl.ds(128 * h + HEAD_DIM, 128 - HEAD_DIM), :] = jnp.zeros((128 - HEAD_DIM, width), bf16)
        for s in range(3):
            heads[s, h, pl.ds(HEAD_DIM, 128 - HEAD_DIM), :] = jnp.zeros((128 - HEAD_DIM, count), bf16)
    seg_rows = jnp.broadcast_to(segment_ref[...], (count, count))
    same = pre_a.at[:, pl.ds(0, count)]
    same[...] = jnp.where(seg_rows == seg_rows.T, 0.0, -1e30)

    for copy in x_copies:
        copy.wait()
    total = jnp.zeros((1, count), f32)
    for b in range(width // 128):
        total += jnp.sum(x_t[pl.ds(128 * b, 128), :].astype(f32), axis=0, keepdims=True)
    mean = total * (1.0 / width)
    total = jnp.zeros((1, count), f32)
    for b in range(width // 128):
        center = x_t[pl.ds(128 * b, 128), :].astype(f32) - mean
        total += jnp.sum(center * center, axis=0, keepdims=True)
    scale = lax.rsqrt(total * (1.0 / width) + 1e-06)
    for b in range(width // 128):
        gain = jnp.broadcast_to(gains_ref[0:1, pl.ds(128 * b, 128)], (128, 128)).T
        gain = jnp.concatenate([gain] * (count // 128), axis=1)
        x = x_t[pl.ds(128 * b, 128), :].astype(f32)
        normed_t[pl.ds(128 * b, 128), :] = ((x - mean) * scale * gain).astype(bf16)

    for s in range(3):
        qkv_copy(s).wait()
        for c in range(2 * s, min(2 * s + 2, middle)):
            up_copy(c).start()
            if c < 3:
                down_copy(c).start()
        product = jnp.dot(qkv_buf[s], normed_t[...], preferred_element_type=f32)
        for h in range(head_count):
            heads[s, h, pl.ds(0, HEAD_DIM), :] = product[HEAD_DIM * h : HEAD_DIM * (h + 1)].astype(bf16)
    down_copy(3).start()

    for h in range(head_count):
        scores = lax.dot_general(
            heads[1, h], heads[0, h], (((0,), (0,)), ((), ())), preferred_element_type=f32
        )
        scores = jnp.where(same[...] == 0.0, scores * HEAD_DIM ** (-0.5), -1e30)
        top = jnp.max(scores, axis=0, keepdims=True)
        expo = jnp.exp(scores - top)
        share = 1.0 / jnp.sum(expo, axis=0, keepdims=True)
        mixed = jnp.dot(heads[2, h], expo.astype(bf16), preferred_element_type=f32) * share
        context[:, pl.ds(128 * h, 128)] = mixed.T.astype(bf16)

    for h in range(head_count):
        wout_copy(h).wait()
    pl.semaphore_wait(barrier, 64)
    swaps = []
    for k, (start, size) in enumerate(cuts):
        cols = pl.ds(start, size)
        product = jnp.dot(context[...], wout_buf[:, cols], preferred_element_type=f32)
        sent[:, cols] = product.astype(bf16)
        swap = remote(sent.at[:, cols], got1.at[:, cols], s1_sems.at[k], r1_sems.at[k])
        swap.start()
        swaps.append(swap)
        resid[:, cols] = product + x_t[cols, :].astype(f32).T

    for c in range(middle, hidden_chunks):
        up_copy(c).start()
        down_copy(c).start()

    for peer in place.others():
        pltpu.make_async_remote_copy(
            src_ref=own_rows.at[peer // 32], dst_ref=table.at[me], send_sem=send_sem_o, recv_sem=recv_sem_o,
            device_id={"req": peer}, device_id_type=MESH,
        ).start()
    table[me] = own_rows[me // 32]

    for swap in swaps:
        swap.wait()

    def norm_to(which, out, extra):
        for b in range(count // 32):
            rows = pl.ds(32 * b, 32)
            x = resid[rows, :] + extra[rows, :].astype(f32)
            resid[rows, :] = x
            center = x - jnp.sum(x, axis=1, keepdims=True) * (1.0 / width)
            spread = jnp.sum(center * center, axis=1, keepdims=True) * (1.0 / width)
            out[rows, :] = (center * lax.rsqrt(spread + 1e-06) * gains_ref[which : which + 1, :]).astype(bf16)

    norm_to(1, normed, got1)

    def up(c, out):
        out[...] = jnp.dot(normed[...], pool[c], preferred_element_type=f32)

    def gelu(pre, out):
        u = pre[...]
        out[...] = (0.5 * u * (1.0 + lax.erf(u * 0.5**0.5))).astype(bf16)

    def down(c, hid):
        product = jnp.dot(hid[...], down_place(c)[...], preferred_element_type=f32)
        acc[...] = product if c == 0 else acc[...] + product

    def wait_chunks(chunks):
        for c in chunks:
            up_copy(c).wait()
            down_copy(c).wait()

    wait_chunks(range(middle))
    for m in range(spare):
        merge_copy(m).start()
    up(0, pre_a)
    up(1, pre_b)
    gelu(pre_a, hid_a)
    for c in range(0, hidden_chunks - 2, 2):
        if c + 2 == middle:
            wait_chunks(range(middle, hidden_chunks))
            for m in range(middle):
                merge_copy(spare + m).start()
        up(c + 2, pre_a)
        gelu(pre_b, hid_b)
        down(c, hid_a)
        up(c + 3, pre_b)
        gelu(pre_a, hid_a)
        down(c + 1, hid_b)

    gelu(pre_b, hid_b)
    swaps = []
    for k, (start, size) in enumerate(cuts):
        cols = pl.ds(start, size)
        product = acc[:, cols] + jnp.dot(
            hid_a[...], down_place(hidden_chunks - 2)[:, cols], preferred_element_type=f32
        )
        product += jnp.dot(
            hid_b[...], down_place(hidden_chunks - 1)[:, cols], preferred_element_type=f32
        )
        sent[:, cols] = product.astype(bf16)
        swap = remote(sent.at[:, cols], got2.at[:, cols], s2_sems.at[k], r2_sems.at[k])
        swap.start()
        swaps.append(swap)
        resid[:, cols] += product
    for m in range(middle, hidden_chunks):
        merge_copy(spare + m).start()

    row = lax.broadcasted_iota(jnp.int32, (count, count), 0)
    token = lax.broadcasted_iota(jnp.int32, (count, count), 1)
    quarter = count // 4
    part, request, rank = row // quarter, lax.rem(row, quarter) // CAP, lax.rem(row, CAP)
    first = jnp.sum((segment_ref[...] < 1).astype(jnp.int32), axis=1, keepdims=True)
    want = request * first + 4 * rank + part
    pick = jnp.where((token == want) & (segment_ref[...] == request), 1.0, 0.0).astype(bf16)

    def all_but_one(ref):
        return ref.at[pl.ds(0, 63)]

    def wait_all(ref, sem):
        pltpu.make_async_copy(all_but_one(ref), all_but_one(ref), sem).wait()

    wait_all(table, recv_sem_o)
    lanes = lax.broadcasted_iota(jnp.int32, (64, 1, 128), 2)
    sources = lax.broadcasted_iota(jnp.int32, (64, 1, 128), 0)
    inv_v[...] = jnp.max(jnp.where(table[...] == lanes, sources, 0), axis=0)
    to_scalar = pltpu.make_async_copy(inv_v, inv_s, inv_sem)
    to_scalar.start()
    to_scalar.wait()

    for swap in swaps:
        swap.wait()
    norm_to(2, normed, got2)
    for i in range(4):
        merged[:, pl.ds(width * i, width)] = jnp.dot(
            pick[quarter * i : quarter * (i + 1)], normed[...], preferred_element_type=f32
        ).astype(bf16)

    for k, dy in enumerate((2, 3, 1, 0)):
        for i in range(4):
            merge_copy(4 * k + i).wait()
        product = jnp.zeros((quarter, hidden_chunk), f32)
        for i in range(4):
            m = 4 * k + i
            product += jnp.dot(
                merged[:, pl.ds(width * i, width)], pool[(hidden_chunks + m) % slots], preferred_element_type=f32
            )
        for g in range(4):
            for x in range(4):
                tiles[g * 16 + place.y[dy] * 4 + x] = product[16 * g : 16 * g + 16, 128 * x : 128 * x + 128].astype(bf16)
        for peer in place.others((dy,)):
            pltpu.make_async_remote_copy(
                src_ref=tiles.at[peer], dst_ref=inbox.at[me], send_sem=send_sem_a, recv_sem=recv_sem_a,
                device_id={"req": peer}, device_id_type=MESH,
            ).start()
    inbox[me] = tiles[me]
    wait_all(inbox, recv_sem_a)

    for d in range(64):
        sorted_tiles[d] = inbox[inv_s[0, d]]
    for peer in place.others():
        pltpu.make_async_remote_copy(
            src_ref=sorted_tiles.at[peer], dst_ref=landed.at[me], send_sem=send_sem_b, recv_sem=recv_sem_b,
            device_id={"req": peer}, device_id_type=MESH,
        ).start()
    landed[me] = sorted_tiles[me]
    wait_all(landed, recv_sem_b)
    for g in range(4):
        for c in range(16):
            out_ref[pl.ds(16 * g, 16), pl.ds(128 * c, 128)] = landed[g * 16 + c]
    wait_all(table, send_sem_o)
    wait_all(tiles, send_sem_a)
    wait_all(sorted_tiles, send_sem_b)


def layer(own, other, segment, owner, qkv_t, w_out, w_up, w_down, gains, w_merge):
    half, count = own.shape
    width = 2 * half
    hidden = w_up.shape[1]
    chunk = 512
    chunks = hidden // chunk
    slots = 16
    heads = half // HEAD_DIM
    rows, out_width = count // 4, w_merge.shape[1]
    f32, bf16 = jnp.float32, jnp.bfloat16
    vmem = pl.BlockSpec(memory_space=pltpu.VMEM)
    hbm = pl.BlockSpec(memory_space=pltpu.HBM)
    dma = pltpu.SemaphoreType.DMA
    return pl.pallas_call(
        layer_kernel,
        out_shape=jax.ShapeDtypeStruct((rows, out_width), bf16),
        in_specs=[hbm] * 10,
        out_specs=vmem,
        scratch_shapes=[
            pltpu.VMEM((width, count), bf16),
            pltpu.VMEM((1, count), jnp.int32),
            pltpu.SMEM((2,), jnp.int32),
            pltpu.VMEM((3, width), f32),
            pltpu.VMEM((3, half, width), bf16),
            pltpu.VMEM((heads * 128, width), bf16),
            pltpu.VMEM((slots, width, chunk), bf16),
            pltpu.VMEM((3, chunk, width), bf16),
            pltpu.VMEM((width, count), bf16),
            pltpu.VMEM((3, heads, 128, count), bf16),
            pltpu.VMEM((count, heads * 128), bf16),
            pltpu.VMEM((count, width), f32),
            pltpu.VMEM((count, width), f32),
            pltpu.VMEM((count, width), bf16),
            pltpu.VMEM((count, chunk), f32),
            pltpu.VMEM((count, chunk), f32),
            pltpu.VMEM((count, chunk), bf16),
            pltpu.VMEM((count, chunk), bf16),
        ]
        + [pltpu.VMEM((count, width), bf16)] * 3
        + [pltpu.VMEM((rows, 4 * width), bf16)]
        + [pltpu.VMEM((64, 16, 128), bf16)] * 4
        + [
            pltpu.VMEM((2, 1, 128), jnp.int32),
            pltpu.VMEM((64, 1, 128), jnp.int32),
            pltpu.VMEM((1, 128), jnp.int32),
            pltpu.SMEM((1, 128), jnp.int32),
        ]
        + [dma((2,)), dma((3,)), dma((3,)), dma((heads,)), dma((slots,)), dma((chunks,))]
        + [dma((3,))] * 4
        + [dma] * 7,
        compiler_params=pltpu.CompilerParams(
            collective_id=2, has_side_effects=True, vmem_limit_bytes=62 * 1024 * 1024
        ),
        name="layer",
    )(own, other, segment, owner, qkv_t, w_out, w_up, w_down, gains, w_merge)


def local(patches, segment, owner, w_qkv, w_out, w_up, w_down, gains, w_merge):
    own = patches.T
    return layer(
        own, swap_halves(own), segment.reshape(1, -1), owner, w_qkv.transpose(0, 2, 1), w_out, w_up, w_down,
        gains, w_merge,
    )


def solution(mesh):
    in_specs = (
        P("req", "tp"),
        P("req"),
        P("req"),
        P(None, None, "tp"),
        P("tp", None),
        P(None, "tp"),
        P("tp", None),
        P(),
        P(None, "tp"),
    )
    out_specs = P("req", "tp")
    return jax.shard_map(local, mesh=mesh, in_specs=in_specs, out_specs=out_specs, check_vma=False)
```
